256 devices in a mesh: seq: 64 (over y, z, core), head: 4 (over x).
Axes of the slice: x: 4, y: 4, z: 8, core: 2. Of those that a mesh axis runs over, the one named last changes fastest.
Arguments:
- queries: bfloat16 [32768, 2048], P('seq', 'head'), may hold values from -6 to 6
- keys: bfloat16 [32768, 2048], P('seq', 'head'), may hold values from -6 to 6
- values: bfloat16 [32768, 2048], P('seq', 'head'), may hold values from -6 to 6
- out_grad: bfloat16 [32768, 4096], P('seq', 'head'), may hold values from -16 to 16
- out_weight: bfloat16 [4096, 2048], P(None, 'head'), may hold values from -0.125 to 0.125
Outputs:
- query_grad: bfloat16 [32768, 2048], P('seq', 'head')
- key_grad: bfloat16 [32768, 2048], P('seq', 'head')
- value_grad: bfloat16 [32768, 2048], P('seq', 'head')
- weight_grad: float32 [4096, 2048], P('seq', 'head')
The draws below stay inside these ranges and needn't reach their ends.
All inputs are finite; a program needn't handle non-finite values.
Results may differ from the reference program's by a relative error of at most 0.0058.
Values may be sent and summed in bfloat16 or wider, within the bound.
A program may use at most 128 MiB of HBM per device.

```python
import math
import jax
import jax.numpy as jnp
from jax import lax

D = 4096
HEADS = 16
HD = 128
TOK_DEV = 512
TOKENS = 32768
N_SEQ = 64


def spiked(array, rng, source, target, blocks, factor):
    def block_of(position):
        return (jnp.arange(array.shape[position]) // (array.shape[position] // blocks)).reshape((-1,) + (1,) * (array.ndim - 1 - position))

    near = jax.random.permutation(rng, blocks)[block_of(target)]
    far = (block_of(target) + blocks // 2) % blocks
    return jnp.where((block_of(source) == near) | (block_of(source) == far), factor * array, array)


def block_levels(key, extent, pieces, least, top_value):
    def one(axis_at, parts):
        heights = jax.random.uniform(jax.random.fold_in(jax.random.fold_in(key, 6), axis_at), (parts,), jnp.float32, least / len(pieces), top_value / len(pieces))
        return jnp.repeat(jnp.exp(heights), extent[axis_at] // parts).reshape((-1,) + (1,) * (len(extent) - axis_at - 1))

    factor_of = one(*pieces[0])
    for cut in pieces[1:]:
        factor_of = factor_of * one(*cut)
    return factor_of


def scatter_about(own_key, dims, scale, bound, cuts=(), dtype=jnp.bfloat16):
    drawn = jax.random.normal(own_key, dims, jnp.float32) * scale
    if len(cuts) > 0:
        drawn = block_levels(own_key, dims, cuts, -0.22, 0.18) * drawn
    return jnp.clip(drawn, min=-bound, max=bound).astype(dtype)


def gaussian_with(key, dims, width, limit, cuts, heavy, dtype=jnp.bfloat16):
    entries = width * jax.random.normal(key, dims, jnp.float32)
    if cuts:
        entries = entries * block_levels(key, dims, cuts, -0.22, 0.18)
    return jnp.clip(spiked(entries, jax.random.fold_in(key, 3), *heavy), -limit, limit).astype(dtype)


def setup_inputs(seed: int = 0) -> dict:
    seeds = jax.random.split(jax.random.key(seed), 6)
    queries = scatter_about(seeds[0], (TOKENS, HEADS * HD), 1.0, 6.0, ((0, 64), (1, 4)))
    keys = scatter_about(seeds[1], (TOKENS, HEADS * HD), 1.0, 6.0, ((0, 64), (1, 4)))
    values = scatter_about(seeds[2], (TOKENS, HEADS * HD), 1.0, 6.0, ((0, 64), (1, 4)))
    out_grad = gaussian_with(seeds[3], (TOKENS, D), 1.0, 16.0, ((0, 64), (1, 4)), (0, 1, 64, 4.0))
    out_weight = scatter_about(seeds[4], (D, HEADS * HD), (HEADS * HD) ** -0.5, 0.125, ((1, 4),))
    return dict(queries=queries, keys=keys, values=values, out_grad=out_grad, out_weight=out_weight)


def reference(queries, keys, values, out_grad, out_weight):
    scale = 1.0 / math.sqrt(HD * TOKENS)
    attn_grad = jnp.dot(out_grad, out_weight, preferred_element_type=jnp.float32).astype(jnp.bfloat16)
    shape = (N_SEQ, TOK_DEV, HEADS, HD)
    q32 = queries.reshape(shape).astype(jnp.float32)
    k32 = keys.reshape(shape).astype(jnp.float32)
    v32 = values.reshape(shape).astype(jnp.float32)
    d32 = attn_grad.reshape(shape).astype(jnp.float32)
    kv_term = scale * jnp.einsum('ntha,nthb->nhab', k32, v32)
    back_term = scale * jnp.einsum('ntha,nthb->nhab', q32, d32)
    zero = jnp.zeros_like(kv_term[:1])
    prior = jnp.concatenate([zero, jnp.cumsum(kv_term, axis=0)[:-1]], axis=0).astype(jnp.bfloat16)
    later_sum = jnp.flip(jnp.cumsum(jnp.flip(back_term, 0), axis=0), 0)
    later = jnp.concatenate([later_sum[1:], zero], axis=0).astype(jnp.bfloat16)
    mask = jnp.tril(jnp.ones((TOK_DEV, TOK_DEV), jnp.float32))

    def block(index):
        q = q32[index]
        k = k32[index]
        v = v32[index]
        d = d32[index]
        pri = prior[index].astype(jnp.float32)
        lat = later[index].astype(jnp.float32)
        probs = (scale * jnp.einsum('tha,sha->hts', q, k) * mask).astype(jnp.bfloat16).astype(jnp.float32)
        grads = (scale * jnp.einsum('thb,shb->hts', d, v) * mask).astype(jnp.bfloat16).astype(jnp.float32)
        outs = (jnp.einsum('hts,shb->thb', probs, v) + jnp.einsum('tha,hab->thb', q, pri)).astype(jnp.bfloat16)
        dq = (jnp.einsum('hts,sha->tha', grads, k) + jnp.einsum('thb,hab->tha', d, pri)).astype(jnp.bfloat16)
        dk = (jnp.einsum('hts,tha->sha', grads, q) + jnp.einsum('shb,hab->sha', v, lat)).astype(jnp.bfloat16)
        dv = (jnp.einsum('hts,thb->shb', probs, d) + jnp.einsum('sha,hab->shb', k, lat)).astype(jnp.bfloat16)
        return (outs, dq, dk, dv)
    outs, dq, dk, dv = lax.map(block, jnp.arange(N_SEQ))
    flat = (TOKENS, HEADS * HD)
    outs = outs.reshape(flat)
    weight_grad = jnp.dot(out_grad.T, outs, preferred_element_type=jnp.float32) * (1.0 / math.sqrt(TOKENS))
    return (dq.reshape(flat), dk.reshape(flat), dv.reshape(flat), weight_grad)
```

```python
import functools
import math

import jax
import jax.numpy as jnp
from jax import lax
from jax.experimental import pallas as pl
from jax.experimental.pallas import tpu as pltpu
from jax.sharding import PartitionSpec as P

HD = 128
NX, NY, NZ = 4, 4, 8
MESH = pl.DeviceIdType.MESH
F32 = jnp.float32
BF16 = jnp.bfloat16


def dotg(a, b, ca, cb):
    return lax.dot_general(a, b, (((ca,), (cb,)), ((), ())), preferred_element_type=F32)


def flag(cond):
    return jnp.where(cond, 1.0, 0.0).astype(F32)


class Place:
    def __init__(self):
        s = lax.axis_index("seq")
        self.x = lax.axis_index("head")
        self.c = s % 2
        self.z = (s // 2) % NZ
        self.y = s // (2 * NZ)

    def at(self, dx=0, dy=0, dz=0, flip=False):
        x = (self.x + dx + NX) % NX
        y = (self.y + dy + NY) % NY
        z = (self.z + dz + NZ) % NZ
        c = 1 - self.c if flip else self.c
        return ((y * NZ + z) * 2 + c, x)


def remote(src, dst, send, recv, device):
    return pltpu.make_async_remote_copy(
        src_ref=src, dst_ref=dst, send_sem=send, recv_sem=recv, device_id=device, device_id_type=MESH
    )


class Scan:
    def __init__(self, here, refs, forward):
        self.here, self.forward = here, forward
        (self.term, self.pbuf, self.own, self.zp, self.zm, self.tot, self.yr, self.fsend, self.out,
         self.base, self.ssem, self.rsem) = refs
        half = self.pbuf.shape[0]
        self.mine = pl.ds(pl.multiple_of(here.c * half, half), half)
        self.theirs = pl.ds(pl.multiple_of((1 - here.c) * half, half), half)
        self.copies = {}

    def copy(self, name, index, src, dst, device):
        made = remote(src, dst, self.ssem.at[index], self.rsem.at[index], device)
        made.start()
        self.copies[name] = made

    def p1_start(self):
        self.copy("p1", 0, self.term.at[self.theirs], self.pbuf, self.here.at(flip=True))

    def p1_wait(self):
        self.copies["p1"].wait_recv()
        self.own[...] = (self.term[self.mine, :] + self.pbuf[...]).astype(BF16)

    def z_start(self, k):
        here = self.here
        self.copy(("p", k), k, self.own if k == 1 else self.zp.at[k - 2], self.zp.at[k - 1], here.at(dz=1))
        if k <= 3:
            self.copy(("m", k), 4 + k, self.own if k == 1 else self.zm.at[k - 2], self.zm.at[k - 1], here.at(dz=-1))

    def z_wait(self, k):
        self.copies[("p", k)].wait_recv()
        if k <= 3:
            self.copies[("m", k)].wait_recv()

    def y_start(self):
        z = self.here.z
        total = self.own[...].astype(F32)
        base = jnp.zeros_like(total)
        for d in range(1, 5):
            v = self.zp[d - 1].astype(F32)
            total = total + v
            base = base + v * flag((z - d >= 0) if self.forward else (z - d < 0))
        for d in range(1, 4):
            v = self.zm[d - 1].astype(F32)
            total = total + v
            base = base + v * flag((z + d >= NZ) if self.forward else (z + d < NZ))
        self.tot[...] = total.astype(BF16)
        self.base[...] = base
        for d in range(1, NY):
            self.copy(("y", d), 7 + d, self.tot, self.yr.at[d - 1], self.here.at(dy=d))

    def p4_start(self):
        y, c = self.here.y, self.here.c
        base = self.base[...]
        for d in range(1, NY):
            self.copies[("y", d)].wait_recv()
            base = base + self.yr[d - 1].astype(F32) * flag((y - d >= 0) if self.forward else (y - d < 0))
        first = flag(c == 0)
        second = 1.0 - first
        mine, other = self.term[self.mine, :], self.pbuf[...]
        if self.forward:
            own, partner = base + second * other, base + first * mine
        else:
            own, partner = base + first * other, base + second * mine
        self.out[self.mine, :] = own.astype(BF16)
        self.fsend[...] = partner.astype(BF16)
        self.copy("p4", 11, self.fsend, self.out.at[self.mine], self.here.at(flip=True))

    def p4_wait(self):
        self.copies["p4"].wait_recv()

    def finish(self):
        for made in self.copies.values():
            made.wait_send()


class Reduce:
    def __init__(self, here, unit, target, refs):
        self.here, self.unit, self.target = here, unit, target
        prod, crecv, zms, zmr, zps, zpr, ysend, self.yrecv, self.keep, ssem, rsem, self.ysem = refs
        self.prod, self.crecv = prod.at[unit], crecv.at[unit]
        self.zms, self.zmr, self.zps, self.zpr = zms.at[unit], zmr.at[unit], zps.at[unit], zpr.at[unit]
        self.ysend = ysend.at[unit]
        self.ssem, self.rsem = ssem.at[unit], rsem.at[unit]
        self.copies = {}

    def copy(self, name, index, src, dst, device):
        made = remote(src, dst, self.ssem.at[index], self.rsem.at[index], device)
        made.start()
        self.copies[name] = made

    def core_start(self):
        self.copy("core", 0, self.prod.at[:, 1 - self.here.c], self.crecv, self.here.at(flip=True))

    def local(self, z):
        return self.prod[z, self.here.c].astype(F32) + self.crecv[z].astype(F32)

    def step(self, k):
        z = self.here.z
        if k == 1:
            self.copies["core"].wait_recv()
        if k > 1:
            self.copies[("m", k - 1)].wait_recv()
        val = self.local((z - (5 - k) + NZ) % NZ)
        if k > 1:
            val = val + self.zmr[k - 2].astype(F32)
        self.zms[k - 1] = val.astype(BF16)
        self.copy(("m", k), k, self.zms.at[k - 1], self.zmr.at[k - 1], self.here.at(dz=-1))
        if k <= 3:
            if k > 1:
                self.copies[("p", k - 1)].wait_recv()
            val = self.local((z + (4 - k)) % NZ)
            if k > 1:
                val = val + self.zpr[k - 2].astype(F32)
            self.zps[k - 1] = val.astype(BF16)
            self.copy(("p", k), 4 + k, self.zps.at[k - 1], self.zpr.at[k - 1], self.here.at(dz=1))

    def ycopy(self):
        d = (self.target - self.here.y + NY) % NY
        slot = (d - 1 + NY) % NY
        return d, remote(
            self.ysend, self.yrecv.at[slot], self.ssem.at[8], self.ysem.at[slot],
            ((self.target * NZ + self.here.z) * 2 + self.here.c, self.here.x),
        )

    def last(self):
        self.copies[("m", 4)].wait_recv()
        self.copies[("p", 3)].wait_recv()
        val = self.local(self.here.z) + self.zmr[3].astype(F32) + self.zpr[2].astype(F32)
        d, made = self.ycopy()

        @pl.when(d == 0)
        def _():
            self.keep[...] = val

        @pl.when(d != 0)
        def _():
            self.ysend[...] = val.astype(BF16)
            made.start()

    def finish(self):
        for made in self.copies.values():
            made.wait_send()
        d, made = self.ycopy()

        @pl.when(d != 0)
        def _():
            made.wait_send()


def kernel(scale, factor, q_hbm, k_hbm, v_hbm, og_hbm, w_hbm, dq_ref, dk_ref, dv_ref, dw_ref,
           q, k, v, w, og, probs, opart, o, dacc, do, dkacc, dvacc, lsem, xssem, xrsem, *rest):
    here = Place()
    rows = q.shape[0]
    half = rows // 2
    heads = q.shape[1] // HD
    scan_k = Scan(here, rest[0:12], True)
    scan_b = Scan(here, rest[12:24], False)
    red_refs = rest[24:]
    upper = here.z >= NZ // 2
    side = jnp.where(upper, 1, -1)
    targets = [here.x, (here.x + side + NX) % NX, (here.x - side + NX) % NX, (here.x + 2) % NX]
    units = [Reduce(here, u, targets[u], red_refs) for u in range(4)]

    loads = [pltpu.make_async_copy(src, dst, lsem.at[n]) for n, (src, dst) in enumerate(
        [(k_hbm, k), (v_hbm, v), (q_hbm, q)]
        + [(og_hbm.at[:, pl.ds(i * half * 2, half * 2)], og.at[0, i]) for i in range(2)]
        + [(w_hbm, w)])]
    for made in loads:
        made.start()

    barrier = pltpu.get_barrier_semaphore()
    peers = [here.at(flip=True), here.at(dx=1), here.at(dx=-1), here.at(dz=1), here.at(dz=-1),
             here.at(dy=1), here.at(dy=2), here.at(dy=3)]
    for peer in peers:
        pl.semaphore_signal(barrier, inc=1, device_id=peer, device_id_type=MESH)
    pl.semaphore_wait(barrier, len(peers))

    cols = [pl.ds(i * half * 2, half * 2) for i in range(2)]
    right, left = here.at(dx=1), here.at(dx=-1)

    def xcopy(n, src, dst, device):
        return remote(src, dst, xssem.at[n], xrsem.at[n], device)

    x0 = xcopy(0, og_hbm.at[:, cols[0]], og.at[1, 0], right)
    x1 = xcopy(1, og_hbm.at[:, cols[1]], og.at[2, 1], left)
    x2 = xcopy(2, og_hbm.at[:, cols[0]], og.at[2, 0], left)
    x3 = xcopy(3, og_hbm.at[:, cols[1]], og.at[1, 1], right)
    x4 = xcopy(4, og.at[1, 0], og.at[3, 0], right)
    x5 = xcopy(5, og.at[2, 1], og.at[3, 1], left)
    for made in (x0, x1, x2, x3):
        made.start()

    def hc(h):
        return slice(h * HD, (h + 1) * HD)

    def blk(i):
        return slice(i * half, (i + 1) * half)

    def masked(s, i):
        t = lax.broadcasted_iota(jnp.int32, s.shape, 0) + i * half
        u = lax.broadcasted_iota(jnp.int32, s.shape, 1)
        return jnp.where(u <= t, s * scale, 0.0).astype(BF16)

    def p_head(h):
        for i in range(2):
            n = (i + 1) * half
            p = masked(dotg(q[blk(i), hc(h)], k[0:n, hc(h)], 1, 1), i)
            probs[h, blk(i), 0:n] = p
            opart[blk(i), hc(h)] = jnp.dot(p, v[0:n, hc(h)], preferred_element_type=F32)

    def g_head(h):
        g0 = masked(dotg(do[blk(0), hc(h)], v[0:half, hc(h)], 1, 1), 0)
        g1 = masked(dotg(do[blk(1), hc(h)], v[:, hc(h)], 1, 1), 1)
        prior = scan_k.out[hc(h), :]
        a = jnp.dot(g0, k[0:half, hc(h)], preferred_element_type=F32)
        dq_ref[blk(0), hc(h)] = (a + dotg(do[blk(0), hc(h)], prior, 1, 1)).astype(BF16)
        a = jnp.dot(g1, k[:, hc(h)], preferred_element_type=F32)
        dq_ref[blk(1), hc(h)] = (a + dotg(do[blk(1), hc(h)], prior, 1, 1)).astype(BF16)
        dkacc[blk(0), hc(h)] = dotg(g0, q[blk(0), hc(h)], 0, 0) + dotg(g1[:, 0:half], q[blk(1), hc(h)], 0, 0)
        dkacc[blk(1), hc(h)] = dotg(g1[:, half:], q[blk(1), hc(h)], 0, 0)
        dvacc[blk(0), hc(h)] = dotg(probs[h, :, 0:half], do[:, hc(h)], 0, 0)
        dvacc[blk(1), hc(h)] = dotg(probs[h, blk(1), half:], do[blk(1), hc(h)], 0, 0)

    def wrow(shift, i):
        return ((here.x + shift + NX) % NX) * 2 + i

    chunks = [((0, 0, 0), (0, 1, 0)), ((1, 0, -1), (2, 1, 1)), ((2, 0, 1), (1, 1, -1)), ((3, 0, 2), (3, 1, 2))]

    def do_unit(u):
        for i in range(2):
            acc = None if u == 0 else dacc[blk(i), :]
            for slot, part, shift in chunks[u]:
                a = jnp.dot(og[slot, part, blk(i), :], w[wrow(shift, part)], preferred_element_type=F32)
                acc = a if acc is None else acc + a
            if u == 3:
                do[blk(i), :] = acc.astype(BF16)
            else:
                dacc[blk(i), :] = acc

    def product(u):
        for slot, part, _ in chunks[u]:
            for i in range(2):
                a = dotg(og[slot, part, :, blk(i)], o[...], 0, 0)
                units[u].prod[pl.ds(part * 4 + i * 2, 2)] = a.reshape(2, 2, 64, rows).astype(BF16)

    for made in loads[:2]:
        made.wait()
    for h in range(heads):
        scan_k.term[hc(h), :] = scale * dotg(k[:, hc(h)], v[:, hc(h)], 0, 0)
    scan_k.p1_start()
    loads[2].wait()
    p_head(0)
    scan_k.p1_wait()
    scan_k.z_start(1)
    p_head(1)
    scan_k.z_wait(1)
    scan_k.z_start(2)
    p_head(2)
    scan_k.z_wait(2)
    scan_k.z_start(3)
    p_head(3)
    scan_k.z_wait(3)
    scan_k.z_start(4)
    for made in loads[3:]:
        made.wait()
    do_unit(0)
    scan_k.z_wait(4)
    scan_k.y_start()
    x0.wait_recv()
    x4.start()
    x1.wait_recv()
    x5.start()
    do_unit(1)
    scan_k.p4_start()
    scan_k.p4_wait()
    for h in range(heads):
        a = jnp.dot(q[:, hc(h)], scan_k.out[hc(h), :], preferred_element_type=F32)
        o[:, hc(h)] = (opart[:, hc(h)] + a).astype(BF16)
    for u in (0, 1):
        product(u)
        units[u].core_start()
    units[0].step(1)
    units[1].step(1)
    x2.wait_recv()
    x3.wait_recv()
    do_unit(2)
    product(2)
    units[2].core_start()
    units[0].step(2)
    units[1].step(2)
    units[2].step(1)
    units[0].step(3)
    units[1].step(3)
    units[2].step(2)
    x4.wait_recv()
    x5.wait_recv()
    do_unit(3)
    for h in range(heads):
        scan_b.term[hc(h), :] = scale * dotg(q[:, hc(h)], do[:, hc(h)], 0, 0)
    scan_b.p1_start()
    product(3)
    units[3].core_start()
    scan_b.p1_wait()
    scan_b.z_start(1)
    units[0].step(4)
    units[1].step(4)
    units[2].step(3)
    units[3].step(1)
    g_head(0)
    scan_b.z_wait(1)
    scan_b.z_start(2)
    units[2].step(4)
    units[3].step(2)
    g_head(1)
    scan_b.z_wait(2)
    scan_b.z_start(3)
    units[3].step(3)
    units[0].last()
    units[1].last()
    g_head(2)
    scan_b.z_wait(3)
    scan_b.z_start(4)
    units[3].step(4)
    units[2].last()
    g_head(3)
    scan_b.z_wait(4)
    scan_b.y_start()
    units[3].last()
    scan_b.p4_start()
    scan_b.p4_wait()
    for h in range(heads):
        later = scan_b.out[hc(h), :]
        dk_ref[:, hc(h)] = (dkacc[:, hc(h)] + dotg(v[:, hc(h)], later, 1, 1)).astype(BF16)
        a = jnp.dot(k[:, hc(h)], later, preferred_element_type=F32)
        dv_ref[:, hc(h)] = (dvacc[:, hc(h)] + a).astype(BF16)
    total = units[0].keep[...]
    for d in range(NY - 1):
        remote(units[0].ysend, units[0].yrecv.at[d], units[0].ssem.at[8], units[0].ysem.at[d], here.at(dy=1)).wait_recv()
        total = total + units[0].yrecv[d].astype(F32)
    dw_ref[...] = total * factor
    for made in (x0, x1, x2, x3, x4, x5):
        made.wait_send()
    scan_k.finish()
    scan_b.finish()
    for unit in units:
        unit.finish()


def per_device(queries, keys, values, out_grad, out_weight):
    rows, width = queries.shape
    feat = out_grad.shape[1]
    total = lax.axis_size("seq") * rows
    scale = 1.0 / math.sqrt(HD * total)
    factor = 1.0 / math.sqrt(total)
    heads = width // HD
    part = feat // 2
    blocks = out_weight.shape[0] // part
    out_rows = out_weight.shape[0] // lax.axis_size("seq")
    sem = pltpu.SemaphoreType.DMA
    state = heads * HD
    scan = [
        pltpu.VMEM((state, HD), F32), pltpu.VMEM((state // 2, HD), F32), pltpu.VMEM((state // 2, HD), BF16),
        pltpu.VMEM((4, state // 2, HD), BF16), pltpu.VMEM((3, state // 2, HD), BF16),
        pltpu.VMEM((state // 2, HD), BF16), pltpu.VMEM((3, state // 2, HD), BF16),
        pltpu.VMEM((state // 2, HD), BF16), pltpu.VMEM((state, HD), BF16), pltpu.VMEM((state // 2, HD), F32),
        sem((12,)), sem((12,)),
    ]
    reduce = [
        pltpu.VMEM((4, NZ, 2, out_rows, width), BF16), pltpu.VMEM((4, NZ, out_rows, width), BF16),
        pltpu.VMEM((4, 4, out_rows, width), BF16), pltpu.VMEM((4, 4, out_rows, width), BF16),
        pltpu.VMEM((4, 3, out_rows, width), BF16), pltpu.VMEM((4, 3, out_rows, width), BF16),
        pltpu.VMEM((4, out_rows, width), BF16), pltpu.VMEM((3, out_rows, width), BF16),
        pltpu.VMEM((out_rows, width), F32), sem((4, 9)), sem((4, 9)), sem((3,)),
    ]
    vm = pl.BlockSpec(memory_space=pltpu.VMEM)
    hbm = pl.BlockSpec(memory_space=pl.ANY)
    grad = jax.ShapeDtypeStruct((rows, width), BF16)
    return pl.pallas_call(
        functools.partial(kernel, scale, factor),
        out_shape=(grad, grad, grad, jax.ShapeDtypeStruct((out_rows, width), F32)),
        in_specs=[hbm] * 5,
        out_specs=(vm, vm, vm, vm),
        scratch_shapes=[
            pltpu.VMEM((rows, width), BF16), pltpu.VMEM((rows, width), BF16), pltpu.VMEM((rows, width), BF16),
            pltpu.VMEM((blocks, part, width), BF16), pltpu.VMEM((4, 2, rows, part), BF16),
            pltpu.VMEM((heads, rows, rows), BF16), pltpu.VMEM((rows, width), F32), pltpu.VMEM((rows, width), BF16),
            pltpu.VMEM((rows, width), F32), pltpu.VMEM((rows, width), BF16),
            pltpu.VMEM((rows, width), F32), pltpu.VMEM((rows, width), F32),
            sem((6,)), sem((6,)), sem((6,)),
        ] + scan + scan + reduce,
        compiler_params=pltpu.CompilerParams(
            collective_id=0, has_side_effects=True, vmem_limit_bytes=60 * 1024 * 1024
        ),
        name="attention_backward",
    )(queries, keys, values, out_grad, out_weight.reshape(blocks, part, width))


def solution(mesh):
    return jax.shard_map(
        per_device,
        mesh=mesh,
        in_specs=(P("seq", "head"), P("seq", "head"), P("seq", "head"), P("seq", "head"), P(None, "head")),
        out_specs=(P("seq", "head"), P("seq", "head"), P("seq", "head"), P("seq", "head")),
        check_vma=False,
    )
```

```python
import functools
import math

import jax
import jax.numpy as jnp
from jax import lax
from jax.experimental import pallas as pl
from jax.experimental.pallas import tpu as pltpu
from jax.sharding import PartitionSpec as P

HD = 128
NX, NY, NZ = 4, 4, 8
MESH = pl.DeviceIdType.MESH
F32 = jnp.float32
BF16 = jnp.bfloat16


def dotg(a, b, ca, cb):
    return lax.dot_general(a, b, (((ca,), (cb,)), ((), ())), preferred_element_type=F32)


def flag(cond):
    return jnp.where(cond, 1.0, 0.0).astype(F32)


class Place:
    def __init__(self):
        s = lax.axis_index("seq")
        self.x = lax.axis_index("head")
        self.c = s % 2
        self.z = (s // 2) % NZ
        self.y = s // (2 * NZ)

    def at(self, dx=0, dy=0, dz=0, flip=False):
        x = (self.x + dx + NX) % NX
        y = (self.y + dy + NY) % NY
        z = (self.z + dz + NZ) % NZ
        c = 1 - self.c if flip else self.c
        return ((y * NZ + z) * 2 + c, x)


def remote(src, dst, send, recv, device):
    return pltpu.make_async_remote_copy(
        src_ref=src, dst_ref=dst, send_sem=send, recv_sem=recv, device_id=device, device_id_type=MESH
    )


class Scan:
    def __init__(self, here, refs, forward):
        self.here, self.forward = here, forward
        (self.term, self.pbuf, self.own, self.zp, self.zm, self.tot, self.yr, self.fsend, self.out,
         self.base, self.ssem, self.rsem) = refs
        self.parts = range(self.pbuf.shape[0])
        self.copies = {}

    def mine(self, j):
        return self.here.c * len(self.parts) + j

    def theirs(self, j):
        return (1 - self.here.c) * len(self.parts) + j

    def copy(self, name, j, index, src, dst, device):
        made = remote(src, dst, self.ssem.at[j, index], self.rsem.at[j, index], device)
        made.start()
        self.copies[name, j] = made

    def p1_start(self, j):
        self.copy("core", j, 0, self.term.at[self.theirs(j)], self.pbuf.at[j], self.here.at(flip=True))

    def z_start(self, j, k):
        here = self.here
        if k == 1:
            self.copies["core", j].wait_recv()
            self.own[j] = (self.term[self.mine(j)] + self.pbuf[j]).astype(self.own.dtype)
            up = down = self.own.at[j]
        else:
            self.copies["p%d" % (k - 1), j].wait_recv()
            up = self.zp.at[j, k - 2]
        self.copy("p%d" % k, j, k, up, self.zp.at[j, k - 1], here.at(dz=1))
        if k > 1:
            self.copies["m%d" % (k - 1), j].wait_recv()
            down = self.zm.at[j, k - 2]
        if k <= 3:
            self.copy("m%d" % k, j, 4 + k, down, self.zm.at[j, k - 1], here.at(dz=-1))

    def z_step(self, k):
        for j in self.parts:
            self.z_start(j, k)

    def y_start(self, j):
        z = self.here.z
        total = self.own[j].astype(F32)
        base = jnp.zeros_like(total)
        for d in range(1, 4):
            v = self.zp[j, d - 1].astype(F32)
            total = total + v
            base = base + v * flag((z - d >= 0) if self.forward else (z - d < 0))
            v = self.zm[j, d - 1].astype(F32)
            total = total + v
            base = base + v * flag((z + d >= NZ) if self.forward else (z + d < NZ))
        self.copies["p4", j].wait_recv()
        v = self.zp[j, 3].astype(F32)
        self.tot[j] = (total + v).astype(self.tot.dtype)
        for d in range(1, NY):
            self.copy("y%d" % d, j, 7 + d, self.tot.at[j], self.yr.at[j, d - 1], self.here.at(dy=d))
        self.base[j] = base + v * flag((z - 4 >= 0) if self.forward else (z - 4 < 0))

    def f_start(self, j):
        y, c = self.here.y, self.here.c
        base = self.base[j]
        for d in range(1, NY):
            self.copies["y%d" % d, j].wait_recv()
            base = base + self.yr[j, d - 1].astype(F32) * flag((y - d >= 0) if self.forward else (y - d < 0))
        first = flag(c == 0)
        second = 1.0 - first
        mine, other = self.term[self.mine(j)], self.pbuf[j]
        if self.forward:
            own, partner = base + second * other, base + first * mine
        else:
            own, partner = base + first * other, base + second * mine
        self.fsend[j] = partner.astype(BF16)
        self.copy("f", j, 11, self.fsend.at[j], self.out.at[self.mine(j)], self.here.at(flip=True))
        self.out[self.mine(j)] = own.astype(BF16)

    def f_wait(self):
        for j in self.parts:
            self.copies["f", j].wait_recv()

    def finish(self):
        for made in self.copies.values():
            made.wait_send()


class Reduce:
    def __init__(self, here, unit, target, refs):
        self.here, self.unit, self.target = here, unit, target
        prod, crecv, zms, zmr, zps, zpr, ysend, self.yrecv, self.keep, ssem, rsem, self.ysem = refs
        self.prod, self.crecv = prod.at[unit], crecv.at[unit]
        self.zms, self.zmr, self.zps, self.zpr = zms.at[unit], zmr.at[unit], zps.at[unit], zpr.at[unit]
        self.ysend = ysend.at[unit]
        self.ssem, self.rsem = ssem.at[unit], rsem.at[unit]
        self.copies = {}

    def copy(self, name, index, src, dst, device):
        made = remote(src, dst, self.ssem.at[index], self.rsem.at[index], device)
        made.start()
        self.copies[name] = made

    def core_start(self):
        self.copy("core", 0, self.prod.at[:, 1 - self.here.c], self.crecv, self.here.at(flip=True))

    def local(self, z):
        return self.prod[z, self.here.c].astype(F32) + self.crecv[z].astype(F32)

    def step(self, k):
        z = self.here.z
        if k == 1:
            self.copies["core"].wait_recv()
        if k > 1:
            self.copies[("m", k - 1)].wait_recv()
        val = self.local((z - (5 - k) + NZ) % NZ)
        if k > 1:
            val = val + self.zmr[k - 2].astype(F32)
        self.zms[k - 1] = val.astype(BF16)
        self.copy(("m", k), k, self.zms.at[k - 1], self.zmr.at[k - 1], self.here.at(dz=-1))
        if k <= 3:
            if k > 1:
                self.copies[("p", k - 1)].wait_recv()
            val = self.local((z + (4 - k)) % NZ)
            if k > 1:
                val = val + self.zpr[k - 2].astype(F32)
            self.zps[k - 1] = val.astype(BF16)
            self.copy(("p", k), 4 + k, self.zps.at[k - 1], self.zpr.at[k - 1], self.here.at(dz=1))

    def ycopy(self):
        d = (self.target - self.here.y + NY) % NY
        slot = (d - 1 + NY) % NY
        return d, remote(
            self.ysend, self.yrecv.at[slot], self.ssem.at[8], self.ysem.at[slot],
            ((self.target * NZ + self.here.z) * 2 + self.here.c, self.here.x),
        )

    def last(self):
        self.copies[("m", 4)].wait_recv()
        self.copies[("p", 3)].wait_recv()
        val = self.local(self.here.z) + self.zmr[3].astype(F32) + self.zpr[2].astype(F32)
        d, made = self.ycopy()

        @pl.when(d == 0)
        def _():
            self.keep[...] = val

        @pl.when(d != 0)
        def _():
            self.ysend[...] = val.astype(BF16)
            made.start()

    def finish(self):
        for made in self.copies.values():
            made.wait_send()
        d, made = self.ycopy()

        @pl.when(d != 0)
        def _():
            made.wait_send()


def kernel(scale, factor, q_hbm, k_hbm, v_hbm, og_hbm, w_hbm, dq_hbm, dk_hbm, dv_hbm, dw_hbm,
           q, k, v, w, og, probs, opart, o, dacc, do, dkacc, dvacc, dq_ref, dk_ref, dv_ref, dw_ref,
           lsem, osem, xssem, xrsem, *rest):
    here = Place()
    rows = q.shape[0]
    half = rows // 2
    heads = q.shape[1] // HD
    scan_k = Scan(here, rest[0:12], True)
    scan_b = Scan(here, rest[12:24], False)
    red_refs = rest[24:]
    upper = here.z >= NZ // 2
    side = jnp.where(upper, 1, -1)
    targets = [here.x, (here.x + side + NX) % NX, (here.x - side + NX) % NX, (here.x + 2) % NX]
    units = [Reduce(here, u, targets[u], red_refs) for u in range(4)]

    loads = [pltpu.make_async_copy(src, dst, lsem.at[n]) for n, (src, dst) in enumerate(
        [(k_hbm, k), (v_hbm, v), (q_hbm, q)]
        + [(og_hbm.at[:, pl.ds(i * half * 2, half * 2)], og.at[0, i]) for i in range(2)]
        + [(w_hbm, w)])]
    for made in loads:
        made.start()

    barrier = pltpu.get_barrier_semaphore()
    peers = [here.at(flip=True), here.at(dx=1), here.at(dx=-1), here.at(dz=1), here.at(dz=-1),
             here.at(dy=1), here.at(dy=2), here.at(dy=3)]
    for peer in peers:
        pl.semaphore_signal(barrier, inc=1, device_id=peer, device_id_type=MESH)
    pl.semaphore_wait(barrier, len(peers))

    cols = [pl.ds(i * half * 2, half * 2) for i in range(2)]
    right, left = here.at(dx=1), here.at(dx=-1)

    def xcopy(n, src, dst, device):
        return remote(src, dst, xssem.at[n], xrsem.at[n], device)

    x0 = xcopy(0, og_hbm.at[:, cols[0]], og.at[1, 0], right)
    x1 = xcopy(1, og_hbm.at[:, cols[1]], og.at[2, 1], left)
    x2 = xcopy(2, og_hbm.at[:, cols[0]], og.at[2, 0], left)
    x3 = xcopy(3, og_hbm.at[:, cols[1]], og.at[1, 1], right)
    x4 = xcopy(4, og.at[1, 0], og.at[3, 0], right)
    x5 = xcopy(5, og.at[2, 1], og.at[3, 1], left)
    for made in (x0, x1, x2, x3):
        made.start()

    def hc(h):
        return slice(h * HD, (h + 1) * HD)

    def blk(i):
        return slice(i * half, (i + 1) * half)

    def masked(s, i):
        t = lax.broadcasted_iota(jnp.int32, s.shape, 0) + i * half
        u = lax.broadcasted_iota(jnp.int32, s.shape, 1)
        return jnp.where(u <= t, s * scale, 0.0).astype(BF16)

    def p_head(h):
        for i in range(2):
            n = (i + 1) * half
            p = masked(dotg(q[blk(i), hc(h)], k[0:n, hc(h)], 1, 1), i)
            probs[h, blk(i), 0:n] = p
            opart[blk(i), hc(h)] = jnp.dot(p, v[0:n, hc(h)], preferred_element_type=F32)

    def g_head(h):
        g0 = masked(dotg(do[blk(0), hc(h)], v[0:half, hc(h)], 1, 1), 0)
        g1 = masked(dotg(do[blk(1), hc(h)], v[:, hc(h)], 1, 1), 1)
        prior = scan_k.out[h]
        a = jnp.dot(g0, k[0:half, hc(h)], preferred_element_type=F32)
        dq_ref[blk(0), hc(h)] = (a + dotg(do[blk(0), hc(h)], prior, 1, 1)).astype(BF16)
        a = jnp.dot(g1, k[:, hc(h)], preferred_element_type=F32)
        dq_ref[blk(1), hc(h)] = (a + dotg(do[blk(1), hc(h)], prior, 1, 1)).astype(BF16)
        dkacc[blk(0), hc(h)] = dotg(g0, q[blk(0), hc(h)], 0, 0) + dotg(g1[:, 0:half], q[blk(1), hc(h)], 0, 0)
        dkacc[blk(1), hc(h)] = dotg(g1[:, half:], q[blk(1), hc(h)], 0, 0)
        dvacc[blk(0), hc(h)] = dotg(probs[h, :, 0:half], do[:, hc(h)], 0, 0)
        dvacc[blk(1), hc(h)] = dotg(probs[h, blk(1), half:], do[blk(1), hc(h)], 0, 0)

    def wrow(shift, i):
        return ((here.x + shift + NX) % NX) * 2 + i

    chunks = [((0, 0, 0), (0, 1, 0)), ((1, 0, -1), (2, 1, 1)), ((2, 0, 1), (1, 1, -1)), ((3, 0, 2), (3, 1, 2))]

    def do_unit(u):
        for i in range(2):
            acc = None if u == 0 else dacc[blk(i), :]
            for slot, part, shift in chunks[u]:
                a = jnp.dot(og[slot, part, blk(i), :], w[wrow(shift, part)], preferred_element_type=F32)
                acc = a if acc is None else acc + a
            if u == 3:
                do[blk(i), :] = acc.astype(BF16)
            else:
                dacc[blk(i), :] = acc

    def product(u):
        for slot, part, _ in chunks[u]:
            for i in range(2):
                a = dotg(og[slot, part, :, blk(i)], o[...], 0, 0)
                units[u].prod[pl.ds(part * 4 + i * 2, 2)] = a.reshape(2, 2, 64, rows).astype(BF16)

    def store(n, src, dst):
        made = pltpu.make_async_copy(src, dst, osem.at[n])
        made.start()
        return made

    for made in loads[:2]:
        made.wait()
    for h in range(heads):
        scan_k.term[h] = scale * dotg(k[:, hc(h)], v[:, hc(h)], 0, 0)
    scan_k.p1_start(0)
    scan_k.p1_start(1)
    loads[2].wait()
    scan_k.z_step(1)
    p_head(0)
    scan_k.z_step(2)
    p_head(1)
    scan_k.z_step(3)
    p_head(2)
    scan_k.z_step(4)
    p_head(3)
    scan_k.y_start(0)
    scan_k.y_start(1)
    for made in loads[3:]:
        made.wait()
    do_unit(0)
    scan_k.f_start(0)
    scan_k.f_start(1)
    x0.wait_recv()
    x4.start()
    x1.wait_recv()
    x5.start()
    scan_k.f_wait()
    for h in range(heads):
        a = jnp.dot(q[:, hc(h)], scan_k.out[h], preferred_element_type=F32)
        o[:, hc(h)] = (opart[:, hc(h)] + a).astype(BF16)
    product(0)
    units[0].core_start()
    product(1)
    units[1].core_start()
    units[0].step(1)
    units[1].step(1)
    do_unit(1)
    units[0].step(2)
    x2.wait_recv()
    x3.wait_recv()
    product(2)
    units[2].core_start()
    units[1].step(2)
    do_unit(2)
    units[0].step(3)
    units[2].step(1)
    units[1].step(3)
    units[0].step(4)
    units[2].step(2)
    units[1].step(4)
    x4.wait_recv()
    x5.wait_recv()
    do_unit(3)
    for h in range(heads):
        scan_b.term[h] = scale * dotg(q[:, hc(h)], do[:, hc(h)], 0, 0)
    scan_b.p1_start(0)
    scan_b.p1_start(1)
    product(3)
    units[3].core_start()
    scan_b.z_step(1)
    units[2].step(3)
    g_head(0)
    units[3].step(1)
    scan_b.z_step(2)
    units[2].step(4)
    g_head(1)
    units[3].step(2)
    scan_b.z_step(3)
    g_head(2)
    units[3].step(3)
    scan_b.z_step(4)
    g_head(3)
    stores = [store(0, dq_ref, dq_hbm)]
    units[3].step(4)
    scan_b.y_start(0)
    scan_b.y_start(1)
    units[0].last()
    units[1].last()
    units[2].last()
    units[3].last()
    scan_b.f_start(0)
    scan_b.f_start(1)
    scan_b.f_wait()
    for h in range(heads):
        later = scan_b.out[h]
        dk_ref[:, hc(h)] = (dkacc[:, hc(h)] + dotg(v[:, hc(h)], later, 1, 1)).astype(BF16)
        a = jnp.dot(k[:, hc(h)], later, preferred_element_type=F32)
        dv_ref[:, hc(h)] = (dvacc[:, hc(h)] + a).astype(BF16)
    stores += [store(1, dk_ref, dk_hbm), store(2, dv_ref, dv_hbm)]
    total = units[0].keep[...]
    for d in range(NY - 1):
        remote(units[0].ysend, units[0].yrecv.at[d], units[0].ssem.at[8], units[0].ysem.at[d], here.at(dy=1)).wait_recv()
        total = total + units[0].yrecv[d].astype(F32)
    dw_ref[...] = total * factor
    stores.append(store(3, dw_ref, dw_hbm))
    for made in (x0, x1, x2, x3, x4, x5):
        made.wait_send()
    scan_k.finish()
    scan_b.finish()
    for unit in units:
        unit.finish()
    for made in stores:
        made.wait()


def settle(*refs):
    n = (len(refs) - 1) // 3
    ins, outs, held, sem = refs[:n], refs[n:2 * n], refs[2 * n:3 * n], refs[3 * n]
    first = [pltpu.make_async_copy(ins[i], held[i], sem.at[0, i]) for i in range(n)]
    second = [pltpu.make_async_copy(held[i], outs[i], sem.at[1, i]) for i in range(n)]
    for made in first:
        made.start()
    for a, b in zip(first, second):
        a.wait()
        b.start()
    for made in second:
        made.wait()


def per_device(queries, keys, values, out_grad, out_weight):
    rows, width = queries.shape
    feat = out_grad.shape[1]
    total = lax.axis_size("seq") * rows
    scale = 1.0 / math.sqrt(HD * total)
    factor = 1.0 / math.sqrt(total)
    heads = width // HD
    part = feat // 2
    blocks = out_weight.shape[0] // part
    out_rows = out_weight.shape[0] // lax.axis_size("seq")
    sem = pltpu.SemaphoreType.DMA
    n = heads // 2

    def scan(dtype):
        return [
            pltpu.VMEM((heads, HD, HD), F32), pltpu.VMEM((n, HD, HD), F32), pltpu.VMEM((n, HD, HD), dtype),
            pltpu.VMEM((n, 4, HD, HD), dtype), pltpu.VMEM((n, 3, HD, HD), dtype), pltpu.VMEM((n, HD, HD), dtype),
            pltpu.VMEM((n, 3, HD, HD), dtype), pltpu.VMEM((n, HD, HD), BF16), pltpu.VMEM((heads, HD, HD), BF16),
            pltpu.VMEM((n, HD, HD), F32), sem((n, 12)), sem((n, 12)),
        ]

    reduce = [
        pltpu.VMEM((4, NZ, 2, out_rows, width), BF16), pltpu.VMEM((4, NZ, out_rows, width), BF16),
        pltpu.VMEM((4, 4, out_rows, width), BF16), pltpu.VMEM((4, 4, out_rows, width), BF16),
        pltpu.VMEM((4, 3, out_rows, width), BF16), pltpu.VMEM((4, 3, out_rows, width), BF16),
        pltpu.VMEM((4, out_rows, width), BF16), pltpu.VMEM((3, out_rows, width), BF16),
        pltpu.VMEM((out_rows, width), F32), sem((4, 9)), sem((4, 9)), sem((3,)),
    ]
    hbm = pl.BlockSpec(memory_space=pl.ANY)
    grad = jax.ShapeDtypeStruct((rows, width), BF16)
    outs = (grad, grad, grad, jax.ShapeDtypeStruct((out_rows, width), F32))
    held = [pltpu.VMEM(a.shape, a.dtype) for a in outs]
    results = pl.pallas_call(
        functools.partial(kernel, scale, factor),
        out_shape=outs,
        in_specs=[hbm] * 5,
        out_specs=[hbm] * 4,
        scratch_shapes=[
            pltpu.VMEM((rows, width), BF16), pltpu.VMEM((rows, width), BF16), pltpu.VMEM((rows, width), BF16),
            pltpu.VMEM((blocks, part, width), BF16), pltpu.VMEM((4, 2, rows, part), BF16),
            pltpu.VMEM((heads, rows, rows), BF16), pltpu.VMEM((rows, width), F32), pltpu.VMEM((rows, width), BF16),
            pltpu.VMEM((rows, width), F32), pltpu.VMEM((rows, width), BF16),
            pltpu.VMEM((rows, width), F32), pltpu.VMEM((rows, width), F32),
        ] + held + [sem((6,)), sem((4,)), sem((6,)), sem((6,))] + scan(BF16) + scan(BF16) + reduce,
        compiler_params=pltpu.CompilerParams(
            collective_id=0, has_side_effects=True, vmem_limit_bytes=60 * 1024 * 1024
        ),
        name="attention_backward",
    )(queries, keys, values, out_grad, out_weight.reshape(blocks, part, width))
    return pl.pallas_call(
        settle,
        out_shape=outs,
        in_specs=[hbm] * 4,
        out_specs=[hbm] * 4,
        scratch_shapes=held + [sem((2, 4))],
        name="settle",
    )(*results)


def solution(mesh):
    return jax.shard_map(
        per_device,
        mesh=mesh,
        in_specs=(P("seq", "head"), P("seq", "head"), P("seq", "head"), P("seq", "head"), P(None, "head")),
        out_specs=(P("seq", "head"), P("seq", "head"), P("seq", "head"), P("seq", "head")),
        check_vma=False,
    )
```

```python
import functools
import math

import jax
import jax.numpy as jnp
from jax import lax
from jax.experimental import pallas as pl
from jax.experimental.pallas import tpu as pltpu
from jax.sharding import PartitionSpec as P

HD = 128
NX, NY, NZ = 4, 4, 8
MESH = pl.DeviceIdType.MESH
F32 = jnp.float32
BF16 = jnp.bfloat16


def dotg(a, b, ca, cb):
    return lax.dot_general(a, b, (((ca,), (cb,)), ((), ())), preferred_element_type=F32)


def flag(cond):
    return jnp.where(cond, 1.0, 0.0).astype(F32)


class Place:
    def __init__(self):
        s = lax.axis_index("seq")
        self.x = lax.axis_index("head")
        self.c = s % 2
        self.z = (s // 2) % NZ
        self.y = s // (2 * NZ)

    def at(self, dx=0, dy=0, dz=0, flip=False):
        x = (self.x + dx + NX) % NX
        y = (self.y + dy + NY) % NY
        z = (self.z + dz + NZ) % NZ
        c = 1 - self.c if flip else self.c
        return ((y * NZ + z) * 2 + c, x)


def remote(src, dst, send, recv, device):
    return pltpu.make_async_remote_copy(
        src_ref=src, dst_ref=dst, send_sem=send, recv_sem=recv, device_id=device, device_id_type=MESH
    )


class Scan:
    def __init__(self, here, refs, forward):
        self.here, self.forward = here, forward
        (self.term, self.pbuf, self.own, self.zp, self.zm, self.tot, self.yr, self.fsend, self.out,
         self.base, self.ssem, self.rsem) = refs
        self.parts = range(self.pbuf.shape[0])
        self.copies = {}

    def mine(self, j):
        return self.here.c * len(self.parts) + j

    def theirs(self, j):
        return (1 - self.here.c) * len(self.parts) + j

    def copy(self, name, j, index, src, dst, device):
        made = remote(src, dst, self.ssem.at[j, index], self.rsem.at[j, index], device)
        made.start()
        self.copies[name, j] = made

    def p1_start(self, j):
        self.copy("core", j, 0, self.term.at[self.theirs(j)], self.pbuf.at[j], self.here.at(flip=True))

    def z_start(self, j, k):
        here = self.here
        if k == 1:
            self.copies["core", j].wait_recv()
            self.own[j] = (self.term[self.mine(j)] + self.pbuf[j]).astype(self.own.dtype)
            up = down = self.own.at[j]
        else:
            self.copies["p%d" % (k - 1), j].wait_recv()
            up = self.zp.at[j, k - 2]
        self.copy("p%d" % k, j, k, up, self.zp.at[j, k - 1], here.at(dz=1))
        if k > 1:
            self.copies["m%d" % (k - 1), j].wait_recv()
            down = self.zm.at[j, k - 2]
        if k <= 3:
            self.copy("m%d" % k, j, 4 + k, down, self.zm.at[j, k - 1], here.at(dz=-1))

    def z_step(self, k):
        for j in self.parts:
            self.z_start(j, k)

    def y_start(self, j):
        z = self.here.z
        total = self.own[j].astype(F32)
        base = jnp.zeros_like(total)
        for d in range(1, 4):
            v = self.zp[j, d - 1].astype(F32)
            total = total + v
            base = base + v * flag((z - d >= 0) if self.forward else (z - d < 0))
            v = self.zm[j, d - 1].astype(F32)
            total = total + v
            base = base + v * flag((z + d >= NZ) if self.forward else (z + d < NZ))
        self.copies["p4", j].wait_recv()
        v = self.zp[j, 3].astype(F32)
        self.tot[j] = (total + v).astype(self.tot.dtype)
        for d in range(1, NY):
            self.copy("y%d" % d, j, 7 + d, self.tot.at[j], self.yr.at[j, d - 1], self.here.at(dy=d))
        self.base[j] = base + v * flag((z - 4 >= 0) if self.forward else (z - 4 < 0))

    def f_start(self, j):
        y, c = self.here.y, self.here.c
        base = self.base[j]
        for d in range(1, NY):
            self.copies["y%d" % d, j].wait_recv()
            base = base + self.yr[j, d - 1].astype(F32) * flag((y - d >= 0) if self.forward else (y - d < 0))
        first = flag(c == 0)
        second = 1.0 - first
        mine, other = self.term[self.mine(j)], self.pbuf[j]
        if self.forward:
            own, partner = base + second * other, base + first * mine
        else:
            own, partner = base + first * other, base + second * mine
        self.fsend[j] = partner.astype(BF16)
        self.copy("f", j, 11, self.fsend.at[j], self.out.at[self.mine(j)], self.here.at(flip=True))
        self.out[self.mine(j)] = own.astype(BF16)

    def f_wait(self):
        for j in self.parts:
            self.copies["f", j].wait_recv()

    def finish(self):
        for made in self.copies.values():
            made.wait_send()


class Reduce:
    def __init__(self, here, unit, target, refs):
        self.here, self.target, self.way = here, target, 1 if unit % 2 == 0 else -1
        prod, crecv, zms, zmr, zps, zpr, ysend, self.yrecv, self.keep, ssem, rsem, self.ysem = refs
        self.prod, self.crecv = prod.at[unit], crecv.at[unit]
        self.zms, self.zmr, self.zps, self.zpr = zms.at[unit], zmr.at[unit], zps.at[unit], zpr.at[unit]
        self.ysend = ysend.at[unit]
        self.ssem, self.rsem = ssem.at[unit], rsem.at[unit]
        self.copies = {}

    def copy(self, name, index, src, dst, device):
        made = remote(src, dst, self.ssem.at[index], self.rsem.at[index], device)
        made.start()
        self.copies[name] = made

    def core_start(self, part):
        n = NZ // 2
        blocks = pl.ds(part * n, n)
        self.copy("core%d" % part, 0 if part == 0 else 9, self.prod.at[blocks, 1 - self.here.c],
                  self.crecv.at[blocks], self.here.at(flip=True))

    def local(self, z):
        return self.prod[z, self.here.c].astype(F32) + self.crecv[z].astype(F32)

    def step(self, k):
        z, way = self.here.z, self.way
        if k == 1:
            self.copies["core0"].wait_recv()
            self.copies["core1"].wait_recv()
        if k > 1:
            self.copies["m%d" % (k - 1)].wait_recv()
        val = self.local((z - way * (5 - k) + NZ) % NZ)
        if k > 1:
            val = val + self.zmr[k - 2].astype(F32)
        self.zms[k - 1] = val.astype(BF16)
        self.copy("m%d" % k, k, self.zms.at[k - 1], self.zmr.at[k - 1], self.here.at(dz=-way))
        if k <= 3:
            if k > 1:
                self.copies["p%d" % (k - 1)].wait_recv()
            val = self.local((z + way * (4 - k) + NZ) % NZ)
            if k > 1:
                val = val + self.zpr[k - 2].astype(F32)
            self.zps[k - 1] = val.astype(BF16)
            self.copy("p%d" % k, 4 + k, self.zps.at[k - 1], self.zpr.at[k - 1], self.here.at(dz=way))

    def ycopy(self):
        d = (self.target - self.here.y + NY) % NY
        slot = (d - 1 + NY) % NY
        return d, remote(
            self.ysend, self.yrecv.at[slot], self.ssem.at[8], self.ysem.at[slot],
            ((self.target * NZ + self.here.z) * 2 + self.here.c, self.here.x),
        )

    def last(self):
        self.copies["m4"].wait_recv()
        self.copies["p3"].wait_recv()
        val = self.local(self.here.z) + self.zmr[3].astype(F32) + self.zpr[2].astype(F32)
        d, made = self.ycopy()

        @pl.when(d == 0)
        def _():
            self.keep[...] = val

        @pl.when(d != 0)
        def _():
            self.ysend[...] = val.astype(BF16)
            made.start()

    def finish(self):
        for made in self.copies.values():
            made.wait_send()
        d, made = self.ycopy()

        @pl.when(d != 0)
        def _():
            made.wait_send()


def kernel(scale, factor, q_hbm, k_hbm, v_hbm, og_hbm, w_hbm, dq_hbm, dk_hbm, dv_hbm, dw_hbm,
           q, k, v, w, og, probs, opart, o, dacc, do, dkacc, dvacc, dq_ref, dk_ref, dv_ref, dw_ref,
           lsem, osem, xssem, xrsem, *rest):
    here = Place()
    rows = q.shape[0]
    half = rows // 2
    heads = q.shape[1] // HD
    scan_k = Scan(here, rest[0:12], True)
    scan_b = Scan(here, rest[12:24], False)
    red_refs = rest[24:]
    upper = here.z >= NZ // 2
    side = jnp.where(upper, 1, -1)
    targets = [here.x, (here.x + side + NX) % NX, (here.x - side + NX) % NX, (here.x + 2) % NX]
    units = [Reduce(here, u, targets[u], red_refs) for u in range(4)]

    loads = [pltpu.make_async_copy(src, dst, lsem.at[n]) for n, (src, dst) in enumerate(
        [(k_hbm, k), (v_hbm, v), (q_hbm, q)]
        + [(og_hbm.at[:, pl.ds(i * half * 2, half * 2)], og.at[0, i]) for i in range(2)]
        + [(w_hbm, w)])]
    for made in loads:
        made.start()

    barrier = pltpu.get_barrier_semaphore()
    peers = [here.at(flip=True), here.at(dx=1), here.at(dx=-1), here.at(dz=1), here.at(dz=-1),
             here.at(dy=1), here.at(dy=2), here.at(dy=3)]
    for peer in peers:
        pl.semaphore_signal(barrier, inc=1, device_id=peer, device_id_type=MESH)
    pl.semaphore_wait(barrier, len(peers))

    cols = [pl.ds(i * half * 2, half * 2) for i in range(2)]
    right, left = here.at(dx=1), here.at(dx=-1)

    def xcopy(n, src, dst, device):
        return remote(src, dst, xssem.at[n], xrsem.at[n], device)

    x0 = xcopy(0, og_hbm.at[:, cols[0]], og.at[1, 0], right)
    x1 = xcopy(1, og_hbm.at[:, cols[1]], og.at[2, 1], left)
    x2 = xcopy(2, og_hbm.at[:, cols[0]], og.at[2, 0], left)
    x3 = xcopy(3, og_hbm.at[:, cols[1]], og.at[1, 1], right)
    x4 = xcopy(4, og.at[1, 0], og.at[3, 0], right)
    x5 = xcopy(5, og.at[2, 1], og.at[3, 1], left)
    for made in (x0, x1, x2, x3):
        made.start()

    def hc(h):
        return slice(h * HD, (h + 1) * HD)

    def blk(i):
        return slice(i * half, (i + 1) * half)

    def masked(s, i):
        t = lax.broadcasted_iota(jnp.int32, s.shape, 0) + i * half
        u = lax.broadcasted_iota(jnp.int32, s.shape, 1)
        return jnp.where(u <= t, s * scale, 0.0).astype(BF16)

    def p_head(h):
        for i in range(2):
            n = (i + 1) * half
            p = masked(dotg(q[blk(i), hc(h)], k[0:n, hc(h)], 1, 1), i)
            probs[h, blk(i), 0:n] = p
            opart[blk(i), hc(h)] = jnp.dot(p, v[0:n, hc(h)], preferred_element_type=F32)

    def g_head(h):
        g0 = masked(dotg(do[blk(0), hc(h)], v[0:half, hc(h)], 1, 1), 0)
        g1 = masked(dotg(do[blk(1), hc(h)], v[:, hc(h)], 1, 1), 1)
        prior = scan_k.out[h]
        a = jnp.dot(g0, k[0:half, hc(h)], preferred_element_type=F32)
        dq_ref[blk(0), hc(h)] = (a + dotg(do[blk(0), hc(h)], prior, 1, 1)).astype(BF16)
        a = jnp.dot(g1, k[:, hc(h)], preferred_element_type=F32)
        dq_ref[blk(1), hc(h)] = (a + dotg(do[blk(1), hc(h)], prior, 1, 1)).astype(BF16)
        dkacc[blk(0), hc(h)] = dotg(g0, q[blk(0), hc(h)], 0, 0) + dotg(g1[:, 0:half], q[blk(1), hc(h)], 0, 0)
        dkacc[blk(1), hc(h)] = dotg(g1[:, half:], q[blk(1), hc(h)], 0, 0)
        dvacc[blk(0), hc(h)] = dotg(probs[h, :, 0:half], do[:, hc(h)], 0, 0)
        dvacc[blk(1), hc(h)] = dotg(probs[h, blk(1), half:], do[blk(1), hc(h)], 0, 0)

    def wrow(shift, i):
        return ((here.x + shift + NX) % NX) * 2 + i

    chunks = [((0, 0, 0), (0, 1, 0)), ((1, 0, -1), (2, 1, 1)), ((2, 0, 1), (1, 1, -1)), ((3, 0, 2), (3, 1, 2))]

    def do_unit(u):
        for i in range(2):
            acc = None if u == 0 else dacc[blk(i), :]
            for slot, part, shift in chunks[u]:
                a = jnp.dot(og[slot, part, blk(i), :], w[wrow(shift, part)], preferred_element_type=F32)
                acc = a if acc is None else acc + a
            if u == 3:
                do[blk(i), :] = acc.astype(BF16)
            else:
                dacc[blk(i), :] = acc

    def product(u):
        for slot, part, _ in chunks[u]:
            for i in range(2):
                a = dotg(og[slot, part, :, blk(i)], o[...], 0, 0)
                units[u].prod[pl.ds(part * 4 + i * 2, 2)] = a.reshape(2, 2, 64, rows).astype(BF16)
            units[u].core_start(part)

    def store(n, src, dst):
        made = pltpu.make_async_copy(src, dst, osem.at[n])
        made.start()
        return made

    for made in loads[:2]:
        made.wait()
    for h in range(heads):
        scan_k.term[h] = scale * dotg(k[:, hc(h)], v[:, hc(h)], 0, 0)
    scan_k.p1_start(0)
    scan_k.p1_start(1)
    loads[2].wait()
    scan_k.z_step(1)
    p_head(0)
    scan_k.z_step(2)
    p_head(1)
    scan_k.z_step(3)
    p_head(2)
    scan_k.z_step(4)
    p_head(3)
    scan_k.y_start(0)
    scan_k.y_start(1)
    for made in loads[3:]:
        made.wait()
    do_unit(0)
    scan_k.f_start(0)
    scan_k.f_start(1)
    x0.wait_recv()
    x4.start()
    x1.wait_recv()
    x5.start()
    scan_k.f_wait()
    for h in range(heads):
        a = jnp.dot(q[:, hc(h)], scan_k.out[h], preferred_element_type=F32)
        o[:, hc(h)] = (opart[:, hc(h)] + a).astype(BF16)
    product(0)
    product(1)
    units[0].step(1)
    do_unit(1)
    units[1].step(1)
    x2.wait_recv()
    x3.wait_recv()
    product(2)
    units[0].step(2)
    units[1].step(2)
    do_unit(2)
    units[2].step(1)
    units[0].step(3)
    units[1].step(3)
    units[2].step(2)
    x4.wait_recv()
    x5.wait_recv()
    do_unit(3)
    for h in range(heads):
        scan_b.term[h] = scale * dotg(q[:, hc(h)], do[:, hc(h)], 0, 0)
    scan_b.p1_start(0)
    scan_b.p1_start(1)
    units[0].step(4)
    units[1].step(4)
    scan_b.z_step(1)
    product(3)
    units[2].step(3)
    scan_b.z_step(2)
    g_head(0)
    units[3].step(1)
    units[0].last()
    units[1].last()
    scan_b.z_step(3)
    units[2].step(4)
    g_head(1)
    units[3].step(2)
    scan_b.z_step(4)
    g_head(2)
    units[3].step(3)
    scan_b.y_start(0)
    scan_b.y_start(1)
    g_head(3)
    stores = [store(0, dq_ref, dq_hbm)]
    units[2].last()
    units[3].step(4)
    scan_b.f_start(0)
    scan_b.f_start(1)
    units[3].last()
    scan_b.f_wait()
    for h in range(heads):
        later = scan_b.out[h]
        dk_ref[:, hc(h)] = (dkacc[:, hc(h)] + dotg(v[:, hc(h)], later, 1, 1)).astype(BF16)
        a = jnp.dot(k[:, hc(h)], later, preferred_element_type=F32)
        dv_ref[:, hc(h)] = (dvacc[:, hc(h)] + a).astype(BF16)
    stores += [store(1, dk_ref, dk_hbm), store(2, dv_ref, dv_hbm)]
    total = units[0].keep[...]
    for d in range(NY - 1):
        remote(units[0].ysend, units[0].yrecv.at[d], units[0].ssem.at[8], units[0].ysem.at[d], here.at(dy=1)).wait_recv()
        total = total + units[0].yrecv[d].astype(F32)
    dw_ref[...] = total * factor
    stores.append(store(3, dw_ref, dw_hbm))
    for made in (x0, x1, x2, x3, x4, x5):
        made.wait_send()
    scan_k.finish()
    scan_b.finish()
    for unit in units:
        unit.finish()
    for made in stores:
        made.wait()


def settle(*refs):
    n = (len(refs) - 1) // 3
    ins, outs, held, sem = refs[:n], refs[n:2 * n], refs[2 * n:3 * n], refs[3 * n]
    first = [pltpu.make_async_copy(ins[i], held[i], sem.at[0, i]) for i in range(n)]
    second = [pltpu.make_async_copy(held[i], outs[i], sem.at[1, i]) for i in range(n)]
    for made in first:
        made.start()
    for a, b in zip(first, second):
        a.wait()
        b.start()
    for made in second:
        made.wait()


def per_device(queries, keys, values, out_grad, out_weight):
    rows, width = queries.shape
    feat = out_grad.shape[1]
    total = lax.axis_size("seq") * rows
    scale = 1.0 / math.sqrt(HD * total)
    factor = 1.0 / math.sqrt(total)
    heads = width // HD
    part = feat // 2
    blocks = out_weight.shape[0] // part
    out_rows = out_weight.shape[0] // lax.axis_size("seq")
    sem = pltpu.SemaphoreType.DMA
    n = heads // 2

    def scan(dtype):
        return [
            pltpu.VMEM((heads, HD, HD), F32), pltpu.VMEM((n, HD, HD), F32), pltpu.VMEM((n, HD, HD), dtype),
            pltpu.VMEM((n, 4, HD, HD), dtype), pltpu.VMEM((n, 3, HD, HD), dtype), pltpu.VMEM((n, HD, HD), dtype),
            pltpu.VMEM((n, 3, HD, HD), dtype), pltpu.VMEM((n, HD, HD), BF16), pltpu.VMEM((heads, HD, HD), BF16),
            pltpu.VMEM((n, HD, HD), F32), sem((n, 12)), sem((n, 12)),
        ]

    reduce = [
        pltpu.VMEM((4, NZ, 2, out_rows, width), BF16), pltpu.VMEM((4, NZ, out_rows, width), BF16),
        pltpu.VMEM((4, 4, out_rows, width), BF16), pltpu.VMEM((4, 4, out_rows, width), BF16),
        pltpu.VMEM((4, 3, out_rows, width), BF16), pltpu.VMEM((4, 3, out_rows, width), BF16),
        pltpu.VMEM((4, out_rows, width), BF16), pltpu.VMEM((3, out_rows, width), BF16),
        pltpu.VMEM((out_rows, width), F32), sem((4, 10)), sem((4, 10)), sem((3,)),
    ]
    hbm = pl.BlockSpec(memory_space=pl.ANY)
    grad = jax.ShapeDtypeStruct((rows, width), BF16)
    outs = (grad, grad, grad, jax.ShapeDtypeStruct((out_rows, width), F32))
    held = [pltpu.VMEM(a.shape, a.dtype) for a in outs]
    results = pl.pallas_call(
        functools.partial(kernel, scale, factor),
        out_shape=outs,
        in_specs=[hbm] * 5,
        out_specs=[hbm] * 4,
        scratch_shapes=[
            pltpu.VMEM((rows, width), BF16), pltpu.VMEM((rows, width), BF16), pltpu.VMEM((rows, width), BF16),
            pltpu.VMEM((blocks, part, width), BF16), pltpu.VMEM((4, 2, rows, part), BF16),
            pltpu.VMEM((heads, rows, rows), BF16), pltpu.VMEM((rows, width), F32), pltpu.VMEM((rows, width), BF16),
            pltpu.VMEM((rows, width), F32), pltpu.VMEM((rows, width), BF16),
            pltpu.VMEM((rows, width), F32), pltpu.VMEM((rows, width), F32),
        ] + held + [sem((6,)), sem((4,)), sem((6,)), sem((6,))] + scan(BF16) + scan(BF16) + reduce,
        compiler_params=pltpu.CompilerParams(
            collective_id=0, has_side_effects=True, vmem_limit_bytes=60 * 1024 * 1024
        ),
        name="attention_backward",
    )(queries, keys, values, out_grad, out_weight.reshape(blocks, part, width))
    return pl.pallas_call(
        settle,
        out_shape=outs,
        in_specs=[hbm] * 4,
        out_specs=[hbm] * 4,
        scratch_shapes=held + [sem((2, 4))],
        name="settle",
    )(*results)


def solution(mesh):
    return jax.shard_map(
        per_device,
        mesh=mesh,
        in_specs=(P("seq", "head"), P("seq", "head"), P("seq", "head"), P("seq", "head"), P(None, "head")),
        out_specs=(P("seq", "head"), P("seq", "head"), P("seq", "head"), P("seq", "head")),
        check_vma=False,
    )
```

```python
import functools
import math

import jax
import jax.numpy as jnp
from jax import lax
from jax.experimental import pallas as pl
from jax.experimental.pallas import tpu as pltpu
from jax.sharding import PartitionSpec as P

HD = 128
NX, NY, NZ = 4, 4, 8
MESH = pl.DeviceIdType.MESH
F32 = jnp.float32
BF16 = jnp.bfloat16


def dotg(a, b, ca, cb):
    return lax.dot_general(a, b, (((ca,), (cb,)), ((), ())), preferred_element_type=F32)


def flag(cond):
    return jnp.where(cond, 1.0, 0.0).astype(F32)


class Place:
    def __init__(self):
        s = lax.axis_index("seq")
        self.x = lax.axis_index("head")
        self.c = s % 2
        self.z = (s // 2) % NZ
        self.y = s // (2 * NZ)

    def at(self, dx=0, dy=0, dz=0, flip=False):
        x = (self.x + dx + NX) % NX
        y = (self.y + dy + NY) % NY
        z = (self.z + dz + NZ) % NZ
        c = 1 - self.c if flip else self.c
        return ((y * NZ + z) * 2 + c, x)


def remote(src, dst, send, recv, device):
    return pltpu.make_async_remote_copy(
        src_ref=src, dst_ref=dst, send_sem=send, recv_sem=recv, device_id=device, device_id_type=MESH
    )


class Scan:
    def __init__(self, here, refs, forward):
        self.here, self.forward = here, forward
        (self.term, self.pbuf, self.own, self.zp, self.zm, self.tot, self.yr, self.fsend, self.out,
         self.base, self.ssem, self.rsem) = refs
        self.parts = range(self.pbuf.shape[0])
        self.copies = {}

    def mine(self, j):
        return self.here.c * len(self.parts) + j

    def theirs(self, j):
        return (1 - self.here.c) * len(self.parts) + j

    def copy(self, name, j, index, src, dst, device):
        made = remote(src, dst, self.ssem.at[j, index], self.rsem.at[j, index], device)
        made.start()
        self.copies[name, j] = made

    def p1_start(self, j):
        self.copy("core", j, 0, self.term.at[self.theirs(j)], self.pbuf.at[j], self.here.at(flip=True))

    def z_start(self, j, k):
        here = self.here
        if k == 1:
            self.copies["core", j].wait_recv()
            self.own[j] = (self.term[self.mine(j)] + self.pbuf[j]).astype(self.own.dtype)
            up = down = self.own.at[j]
        else:
            self.copies["p%d" % (k - 1), j].wait_recv()
            up = self.zp.at[j, k - 2]
        self.copy("p%d" % k, j, k, up, self.zp.at[j, k - 1], here.at(dz=1))
        if k > 1:
            self.copies["m%d" % (k - 1), j].wait_recv()
            down = self.zm.at[j, k - 2]
        if k <= 3:
            self.copy("m%d" % k, j, 4 + k, down, self.zm.at[j, k - 1], here.at(dz=-1))

    def z_step(self, k):
        for j in self.parts:
            self.z_start(j, k)

    def y_start(self, j):
        z = self.here.z
        total = self.own[j].astype(F32)
        base = jnp.zeros_like(total)
        for d in range(1, 4):
            v = self.zp[j, d - 1].astype(F32)
            total = total + v
            base = base + v * flag((z - d >= 0) if self.forward else (z - d < 0))
            v = self.zm[j, d - 1].astype(F32)
            total = total + v
            base = base + v * flag((z + d >= NZ) if self.forward else (z + d < NZ))
        self.copies["p4", j].wait_recv()
        v = self.zp[j, 3].astype(F32)
        self.tot[j] = (total + v).astype(self.tot.dtype)
        for d in range(1, NY):
            self.copy("y%d" % d, j, 7 + d, self.tot.at[j], self.yr.at[j, d - 1], self.here.at(dy=d))
        self.base[j] = base + v * flag((z - 4 >= 0) if self.forward else (z - 4 < 0))

    def f_start(self, j):
        y, c = self.here.y, self.here.c
        base = self.base[j]
        for d in range(1, NY):
            self.copies["y%d" % d, j].wait_recv()
            base = base + self.yr[j, d - 1].astype(F32) * flag((y - d >= 0) if self.forward else (y - d < 0))
        first = flag(c == 0)
        second = 1.0 - first
        mine, other = self.term[self.mine(j)], self.pbuf[j]
        if self.forward:
            own, partner = base + second * other, base + first * mine
        else:
            own, partner = base + first * other, base + second * mine
        self.fsend[j] = partner.astype(BF16)
        self.copy("f", j, 11, self.fsend.at[j], self.out.at[self.mine(j)], self.here.at(flip=True))
        self.out[self.mine(j)] = own.astype(BF16)

    def f_wait(self):
        for j in self.parts:
            self.copies["f", j].wait_recv()

    def finish(self):
        for made in self.copies.values():
            made.wait_send()


class Reduce:
    def __init__(self, here, unit, target, refs):
        self.here, self.target, self.way = here, target, 1 if unit % 2 == 0 else -1
        prod, crecv, zms, zmr, zps, zpr, ysend, self.yrecv, self.keep, ssem, rsem, self.ysem = refs
        self.prod, self.crecv = prod.at[unit], crecv.at[unit]
        self.zms, self.zmr, self.zps, self.zpr = zms.at[unit], zmr.at[unit], zps.at[unit], zpr.at[unit]
        self.ysend = ysend.at[unit]
        self.wide = zms.shape[-1]
        self.ssem, self.rsem = ssem.at[unit], rsem.at[unit]
        self.copies = {}

    def copy(self, name, index, src, dst, device):
        made = remote(src, dst, self.ssem.at[index], self.rsem.at[index], device)
        made.start()
        self.copies[name] = made

    def core_start(self, part):
        n = NZ // 2
        blocks = pl.ds(part * n, n)
        self.copy("core%d" % part, part, self.prod.at[blocks, 1 - self.here.c],
                  self.crecv.at[blocks], self.here.at(flip=True))

    def local(self, z, j):
        cols = slice(j * self.wide, (j + 1) * self.wide)
        return self.prod[z, self.here.c, :, cols].astype(F32) + self.crecv[z, :, cols].astype(F32)

    def send(self, name, k, j, index, dest, held, got, way):
        val = self.local(dest, j)
        if k > 1:
            self.copies["%s%d" % (name, k - 1), j].wait_recv()
            val = val + got[k - 2, j].astype(F32)
        held[k - 1, j] = val.astype(BF16)
        made = remote(held.at[k - 1, j], got.at[k - 1, j], self.ssem.at[index], self.rsem.at[index], self.here.at(dz=way))
        made.start()
        self.copies["%s%d" % (name, k), j] = made

    def step(self, k):
        z, way = self.here.z, self.way
        if k == 1:
            self.copies["core0"].wait_recv()
            self.copies["core1"].wait_recv()
        for j in range(2):
            self.send("m", k, j, 1 + k + 8 * j, (z - way * (5 - k) + NZ) % NZ, self.zms, self.zmr, -way)
            if k <= 3:
                self.send("p", k, j, 5 + k + 8 * j, (z + way * (4 - k) + NZ) % NZ, self.zps, self.zpr, way)

    def ycopy(self):
        d = (self.target - self.here.y + NY) % NY
        slot = (d - 1 + NY) % NY
        return d, remote(
            self.ysend, self.yrecv.at[slot], self.ssem.at[18], self.ysem.at[slot],
            ((self.target * NZ + self.here.z) * 2 + self.here.c, self.here.x),
        )

    def last(self):
        vals = []
        for j in range(2):
            self.copies["m4", j].wait_recv()
            self.copies["p3", j].wait_recv()
            vals.append(self.local(self.here.z, j) + self.zmr[3, j].astype(F32) + self.zpr[2, j].astype(F32))
        val = jnp.concatenate(vals, axis=1)
        d, made = self.ycopy()

        @pl.when(d == 0)
        def _():
            self.keep[...] = val

        @pl.when(d != 0)
        def _():
            self.ysend[...] = val.astype(BF16)
            made.start()

    def finish(self):
        for made in self.copies.values():
            made.wait_send()
        d, made = self.ycopy()

        @pl.when(d != 0)
        def _():
            made.wait_send()


def kernel(scale, factor, q_hbm, k_hbm, v_hbm, og_hbm, w_hbm, dq_hbm, dk_hbm, dv_hbm, dw_hbm,
           q, k, v, w, og, probs, opart, o, dacc, do, dkacc, dvacc, dq_ref, dk_ref, dv_ref, dw_ref,
           lsem, osem, xssem, xrsem, *rest):
    here = Place()
    rows = q.shape[0]
    half = rows // 2
    heads = q.shape[1] // HD
    scan_k = Scan(here, rest[0:12], True)
    scan_b = Scan(here, rest[12:24], False)
    red_refs = rest[24:]
    upper = here.z >= NZ // 2
    side = jnp.where(upper, 1, -1)
    targets = [here.x, (here.x + side + NX) % NX, (here.x - side + NX) % NX, (here.x + 2) % NX]
    units = [Reduce(here, u, targets[u], red_refs) for u in range(4)]

    loads = [pltpu.make_async_copy(src, dst, lsem.at[n]) for n, (src, dst) in enumerate(
        [(k_hbm, k), (v_hbm, v), (q_hbm, q)]
        + [(og_hbm.at[:, pl.ds(i * half * 2, half * 2)], og.at[0, i]) for i in range(2)]
        + [(w_hbm, w)])]
    for made in loads:
        made.start()

    barrier = pltpu.get_barrier_semaphore()
    peers = [here.at(flip=True), here.at(dx=1), here.at(dx=-1), here.at(dz=1), here.at(dz=-1),
             here.at(dy=1), here.at(dy=2), here.at(dy=3)]
    for peer in peers:
        pl.semaphore_signal(barrier, inc=1, device_id=peer, device_id_type=MESH)
    pl.semaphore_wait(barrier, len(peers))

    cols = [pl.ds(i * half * 2, half * 2) for i in range(2)]
    right, left = here.at(dx=1), here.at(dx=-1)

    def xcopy(n, src, dst, device):
        return remote(src, dst, xssem.at[n], xrsem.at[n], device)

    x0 = xcopy(0, og_hbm.at[:, cols[0]], og.at[1, 0], right)
    x1 = xcopy(1, og_hbm.at[:, cols[1]], og.at[2, 1], left)
    x2 = xcopy(2, og_hbm.at[:, cols[0]], og.at[2, 0], left)
    x3 = xcopy(3, og_hbm.at[:, cols[1]], og.at[1, 1], right)
    x4 = xcopy(4, og.at[1, 0], og.at[3, 0], right)
    x5 = xcopy(5, og.at[2, 1], og.at[3, 1], left)
    for made in (x0, x1, x2, x3):
        made.start()

    def hc(h):
        return slice(h * HD, (h + 1) * HD)

    def blk(i):
        return slice(i * half, (i + 1) * half)

    def masked(s, i):
        t = lax.broadcasted_iota(jnp.int32, s.shape, 0) + i * half
        u = lax.broadcasted_iota(jnp.int32, s.shape, 1)
        return jnp.where(u <= t, s * scale, 0.0).astype(BF16)

    def p_head(h):
        for i in range(2):
            n = (i + 1) * half
            p = masked(dotg(q[blk(i), hc(h)], k[0:n, hc(h)], 1, 1), i)
            probs[h, blk(i), 0:n] = p
            opart[blk(i), hc(h)] = jnp.dot(p, v[0:n, hc(h)], preferred_element_type=F32)

    def g_head(h):
        g0 = masked(dotg(do[blk(0), hc(h)], v[0:half, hc(h)], 1, 1), 0)
        g1 = masked(dotg(do[blk(1), hc(h)], v[:, hc(h)], 1, 1), 1)
        prior = scan_k.out[h]
        a = jnp.dot(g0, k[0:half, hc(h)], preferred_element_type=F32)
        dq_ref[blk(0), hc(h)] = (a + dotg(do[blk(0), hc(h)], prior, 1, 1)).astype(BF16)
        a = jnp.dot(g1, k[:, hc(h)], preferred_element_type=F32)
        dq_ref[blk(1), hc(h)] = (a + dotg(do[blk(1), hc(h)], prior, 1, 1)).astype(BF16)
        dkacc[blk(0), hc(h)] = dotg(g0, q[blk(0), hc(h)], 0, 0) + dotg(g1[:, 0:half], q[blk(1), hc(h)], 0, 0)
        dkacc[blk(1), hc(h)] = dotg(g1[:, half:], q[blk(1), hc(h)], 0, 0)
        dvacc[blk(0), hc(h)] = dotg(probs[h, :, 0:half], do[:, hc(h)], 0, 0)
        dvacc[blk(1), hc(h)] = dotg(probs[h, blk(1), half:], do[blk(1), hc(h)], 0, 0)

    def wrow(shift, i):
        return ((here.x + shift + NX) % NX) * 2 + i

    chunks = [((0, 0, 0), (0, 1, 0)), ((1, 0, -1), (2, 1, 1)), ((2, 0, 1), (1, 1, -1)), ((3, 0, 2), (3, 1, 2))]

    def do_unit(u):
        for i in range(2):
            acc = None if u == 0 else dacc[blk(i), :]
            for slot, part, shift in chunks[u]:
                a = jnp.dot(og[slot, part, blk(i), :], w[wrow(shift, part)], preferred_element_type=F32)
                acc = a if acc is None else acc + a
            if u == 3:
                do[blk(i), :] = acc.astype(BF16)
            else:
                dacc[blk(i), :] = acc

    def product(u):
        for slot, part, _ in chunks[u]:
            for i in range(2):
                a = dotg(og[slot, part, :, blk(i)], o[...], 0, 0)
                units[u].prod[pl.ds(part * 4 + i * 2, 2)] = a.reshape(2, 2, 64, rows).astype(BF16)
            units[u].core_start(part)

    def store(n, src, dst):
        made = pltpu.make_async_copy(src, dst, osem.at[n])
        made.start()
        return made

    for made in loads[:2]:
        made.wait()
    for h in range(heads):
        scan_k.term[h] = scale * dotg(k[:, hc(h)], v[:, hc(h)], 0, 0)
    scan_k.p1_start(0)
    scan_k.p1_start(1)
    loads[2].wait()
    scan_k.z_step(1)
    p_head(0)
    scan_k.z_step(2)
    p_head(1)
    scan_k.z_step(3)
    p_head(2)
    scan_k.z_step(4)
    p_head(3)
    scan_k.y_start(0)
    scan_k.y_start(1)
    for made in loads[3:]:
        made.wait()
    do_unit(0)
    scan_k.f_start(0)
    scan_k.f_start(1)
    x0.wait_recv()
    x4.start()
    x1.wait_recv()
    x5.start()
    scan_k.f_wait()
    for h in range(heads):
        a = jnp.dot(q[:, hc(h)], scan_k.out[h], preferred_element_type=F32)
        o[:, hc(h)] = (opart[:, hc(h)] + a).astype(BF16)
    product(0)
    product(1)
    units[0].step(1)
    do_unit(1)
    units[1].step(1)
    x2.wait_recv()
    x3.wait_recv()
    product(2)
    units[0].step(2)
    units[1].step(2)
    do_unit(2)
    units[2].step(1)
    units[0].step(3)
    units[1].step(3)
    units[2].step(2)
    x4.wait_recv()
    x5.wait_recv()
    do_unit(3)
    for h in range(heads):
        scan_b.term[h] = scale * dotg(q[:, hc(h)], do[:, hc(h)], 0, 0)
    scan_b.p1_start(0)
    scan_b.p1_start(1)
    product(3)
    scan_b.z_step(1)
    units[0].step(4)
    units[1].step(4)
    units[2].step(3)
    units[3].step(1)
    scan_b.z_step(2)
    g_head(0)
    units[0].last()
    units[1].last()
    units[3].step(2)
    scan_b.z_step(3)
    units[2].step(4)
    g_head(1)
    units[3].step(3)
    scan_b.z_step(4)
    units[2].last()
    g_head(2)
    scan_b.y_start(0)
    scan_b.y_start(1)
    units[3].step(4)
    g_head(3)
    stores = [store(0, dq_ref, dq_hbm)]
    units[3].last()
    scan_b.f_start(0)
    scan_b.f_start(1)
    scan_b.f_wait()
    for h in range(heads):
        later = scan_b.out[h]
        dk_ref[:, hc(h)] = (dkacc[:, hc(h)] + dotg(v[:, hc(h)], later, 1, 1)).astype(BF16)
        a = jnp.dot(k[:, hc(h)], later, preferred_element_type=F32)
        dv_ref[:, hc(h)] = (dvacc[:, hc(h)] + a).astype(BF16)
    stores += [store(1, dk_ref, dk_hbm), store(2, dv_ref, dv_hbm)]
    total = units[0].keep[...]
    for d in range(NY - 1):
        remote(units[0].ysend, units[0].yrecv.at[d], units[0].ssem.at[18], units[0].ysem.at[d], here.at(dy=1)).wait_recv()
        total = total + units[0].yrecv[d].astype(F32)
    dw_ref[...] = total * factor
    stores.append(store(3, dw_ref, dw_hbm))
    for made in (x0, x1, x2, x3, x4, x5):
        made.wait_send()
    scan_k.finish()
    scan_b.finish()
    for unit in units:
        unit.finish()
    for made in stores:
        made.wait()


def settle(*refs):
    n = (len(refs) - 1) // 3
    ins, outs, held, sem = refs[:n], refs[n:2 * n], refs[2 * n:3 * n], refs[3 * n]
    first = [pltpu.make_async_copy(ins[i], held[i], sem.at[0, i]) for i in range(n)]
    second = [pltpu.make_async_copy(held[i], outs[i], sem.at[1, i]) for i in range(n)]
    for made in first:
        made.start()
    for a, b in zip(first, second):
        a.wait()
        b.start()
    for made in second:
        made.wait()


def per_device(queries, keys, values, out_grad, out_weight):
    rows, width = queries.shape
    feat = out_grad.shape[1]
    total = lax.axis_size("seq") * rows
    scale = 1.0 / math.sqrt(HD * total)
    factor = 1.0 / math.sqrt(total)
    heads = width // HD
    part = feat // 2
    blocks = out_weight.shape[0] // part
    out_rows = out_weight.shape[0] // lax.axis_size("seq")
    sem = pltpu.SemaphoreType.DMA
    n = heads // 2

    def scan(dtype):
        return [
            pltpu.VMEM((heads, HD, HD), F32), pltpu.VMEM((n, HD, HD), F32), pltpu.VMEM((n, HD, HD), dtype),
            pltpu.VMEM((n, 4, HD, HD), dtype), pltpu.VMEM((n, 3, HD, HD), dtype), pltpu.VMEM((n, HD, HD), dtype),
            pltpu.VMEM((n, 3, HD, HD), dtype), pltpu.VMEM((n, HD, HD), BF16), pltpu.VMEM((heads, HD, HD), BF16),
            pltpu.VMEM((n, HD, HD), F32), sem((n, 12)), sem((n, 12)),
        ]

    reduce = [
        pltpu.VMEM((4, NZ, 2, out_rows, width), BF16), pltpu.VMEM((4, NZ, out_rows, width), BF16),
        pltpu.VMEM((4, 4, 2, out_rows, width // 2), BF16), pltpu.VMEM((4, 4, 2, out_rows, width // 2), BF16),
        pltpu.VMEM((4, 3, 2, out_rows, width // 2), BF16), pltpu.VMEM((4, 3, 2, out_rows, width // 2), BF16),
        pltpu.VMEM((4, out_rows, width), BF16), pltpu.VMEM((3, out_rows, width), BF16),
        pltpu.VMEM((out_rows, width), F32), sem((4, 19)), sem((4, 19)), sem((3,)),
    ]
    hbm = pl.BlockSpec(memory_space=pl.ANY)
    grad = jax.ShapeDtypeStruct((rows, width), BF16)
    outs = (grad, grad, grad, jax.ShapeDtypeStruct((out_rows, width), F32))
    held = [pltpu.VMEM(a.shape, a.dtype) for a in outs]
    results = pl.pallas_call(
        functools.partial(kernel, scale, factor),
        out_shape=outs,
        in_specs=[hbm] * 5,
        out_specs=[hbm] * 4,
        scratch_shapes=[
            pltpu.VMEM((rows, width), BF16), pltpu.VMEM((rows, width), BF16), pltpu.VMEM((rows, width), BF16),
            pltpu.VMEM((blocks, part, width), BF16), pltpu.VMEM((4, 2, rows, part), BF16),
            pltpu.VMEM((heads, rows, rows), BF16), pltpu.VMEM((rows, width), F32), pltpu.VMEM((rows, width), BF16),
            pltpu.VMEM((rows, width), F32), pltpu.VMEM((rows, width), BF16),
            pltpu.VMEM((rows, width), F32), pltpu.VMEM((rows, width), F32),
        ] + held + [sem((6,)), sem((4,)), sem((6,)), sem((6,))] + scan(BF16) + scan(BF16) + reduce,
        compiler_params=pltpu.CompilerParams(
            collective_id=0, has_side_effects=True, vmem_limit_bytes=60 * 1024 * 1024
        ),
        name="attention_backward",
    )(queries, keys, values, out_grad, out_weight.reshape(blocks, part, width))
    return pl.pallas_call(
        settle,
        out_shape=outs,
        in_specs=[hbm] * 4,
        out_specs=[hbm] * 4,
        scratch_shapes=held + [sem((2, 4))],
        name="settle",
    )(*results)


def solution(mesh):
    return jax.shard_map(
        per_device,
        mesh=mesh,
        in_specs=(P("seq", "head"), P("seq", "head"), P("seq", "head"), P("seq", "head"), P(None, "head")),
        out_specs=(P("seq", "head"), P("seq", "head"), P("seq", "head"), P("seq", "head")),
        check_vma=False,
    )
```

```python
import functools
import math

import jax
import jax.numpy as jnp
from jax import lax
from jax.experimental import pallas as pl
from jax.experimental.pallas import tpu as pltpu
from jax.sharding import PartitionSpec as P

HD = 128
NX, NY, NZ = 4, 4, 8
MESH = pl.DeviceIdType.MESH
F32 = jnp.float32
BF16 = jnp.bfloat16


def dotg(a, b, ca, cb):
    return lax.dot_general(a, b, (((ca,), (cb,)), ((), ())), preferred_element_type=F32)


def flag(cond):
    return jnp.where(cond, 1.0, 0.0).astype(F32)


class Place:
    def __init__(self):
        s = lax.axis_index("seq")
        self.x = lax.axis_index("head")
        self.c = s % 2
        self.z = (s // 2) % NZ
        self.y = s // (2 * NZ)

    def at(self, dx=0, dy=0, dz=0, flip=False):
        x = (self.x + dx + NX) % NX
        y = (self.y + dy + NY) % NY
        z = (self.z + dz + NZ) % NZ
        c = 1 - self.c if flip else self.c
        return ((y * NZ + z) * 2 + c, x)


def remote(src, dst, send, recv, device):
    return pltpu.make_async_remote_copy(
        src_ref=src, dst_ref=dst, send_sem=send, recv_sem=recv, device_id=device, device_id_type=MESH
    )


class Scan:
    def __init__(self, here, refs, forward):
        self.here, self.forward = here, forward
        (self.term, self.pbuf, self.own, self.zp, self.zm, self.tot, self.yr, self.fsend, self.out,
         self.base, self.ssem, self.rsem) = refs
        self.parts = range(self.pbuf.shape[0])
        self.copies = {}

    def mine(self, j):
        return self.here.c * len(self.parts) + j

    def theirs(self, j):
        return (1 - self.here.c) * len(self.parts) + j

    def copy(self, name, j, index, src, dst, device):
        made = remote(src, dst, self.ssem.at[j, index], self.rsem.at[j, index], device)
        made.start()
        self.copies[name, j] = made

    def p1_start(self, j):
        self.copy("core", j, 0, self.term.at[self.theirs(j)], self.pbuf.at[j], self.here.at(flip=True))

    def z_start(self, j, k):
        here = self.here
        if k == 1:
            self.copies["core", j].wait_recv()
            self.own[j] = (self.term[self.mine(j)] + self.pbuf[j]).astype(self.own.dtype)
            up = down = self.own.at[j]
        else:
            self.copies["p%d" % (k - 1), j].wait_recv()
            up = self.zp.at[j, k - 2]
        self.copy("p%d" % k, j, k, up, self.zp.at[j, k - 1], here.at(dz=1))
        if k > 1:
            self.copies["m%d" % (k - 1), j].wait_recv()
            down = self.zm.at[j, k - 2]
        if k <= 3:
            self.copy("m%d" % k, j, 4 + k, down, self.zm.at[j, k - 1], here.at(dz=-1))

    def z_step(self, k):
        for j in self.parts:
            self.z_start(j, k)

    def y_start(self, j):
        z = self.here.z
        total = self.own[j].astype(F32)
        base = jnp.zeros_like(total)
        for d in range(1, 4):
            v = self.zp[j, d - 1].astype(F32)
            total = total + v
            base = base + v * flag((z - d >= 0) if self.forward else (z - d < 0))
            v = self.zm[j, d - 1].astype(F32)
            total = total + v
            base = base + v * flag((z + d >= NZ) if self.forward else (z + d < NZ))
        self.copies["p4", j].wait_recv()
        v = self.zp[j, 3].astype(F32)
        self.tot[j] = (total + v).astype(self.tot.dtype)
        for d in (2, 1, 3):
            self.copy("y%d" % d, j, 7 + d, self.tot.at[j], self.yr.at[j, d - 1], self.here.at(dy=d))
        self.base[j] = base + v * flag((z - 4 >= 0) if self.forward else (z - 4 < 0))

    def f_start(self, j):
        y, c = self.here.y, self.here.c
        base = self.base[j]
        for d in range(1, NY):
            self.copies["y%d" % d, j].wait_recv()
            base = base + self.yr[j, d - 1].astype(F32) * flag((y - d >= 0) if self.forward else (y - d < 0))
        first = flag(c == 0)
        second = 1.0 - first
        mine, other = self.term[self.mine(j)], self.pbuf[j]
        if self.forward:
            own, partner = base + second * other, base + first * mine
        else:
            own, partner = base + first * other, base + second * mine
        self.fsend[j] = partner.astype(BF16)
        self.copy("f", j, 11, self.fsend.at[j], self.out.at[self.mine(j)], self.here.at(flip=True))
        self.out[self.mine(j)] = own.astype(BF16)

    def f_wait(self):
        for j in self.parts:
            self.copies["f", j].wait_recv()

    def finish(self):
        for made in self.copies.values():
            made.wait_send()


class Reduce:
    def __init__(self, here, unit, target, refs):
        self.here, self.target, self.way = here, target, 1 if unit % 2 == 0 else -1
        prod, crecv, zms, zmr, zps, zpr, ysend, self.yrecv, self.keep, ssem, rsem, self.ysem = refs
        self.prod, self.crecv = prod.at[unit], crecv.at[unit]
        self.zms, self.zmr, self.zps, self.zpr = zms.at[unit], zmr.at[unit], zps.at[unit], zpr.at[unit]
        self.ysend = ysend.at[unit]
        self.ssem, self.rsem = ssem.at[unit], rsem.at[unit]
        self.copies = {}

    def copy(self, name, index, src, dst, device):
        made = remote(src, dst, self.ssem.at[index], self.rsem.at[index], device)
        made.start()
        self.copies[name] = made

    def core_start(self, part):
        n = NZ // 2
        blocks = pl.ds(part * n, n)
        self.copy("core%d" % part, 0 if part == 0 else 9, self.prod.at[blocks, 1 - self.here.c],
                  self.crecv.at[blocks], self.here.at(flip=True))

    def local(self, z):
        return self.prod[z, self.here.c].astype(F32) + self.crecv[z].astype(F32)

    def step(self, k):
        z, way = self.here.z, self.way
        if k == 1:
            self.copies["core0"].wait_recv()
            self.copies["core1"].wait_recv()
        if k > 1:
            self.copies["m%d" % (k - 1)].wait_recv()
        val = self.local((z - way * (5 - k) + NZ) % NZ)
        if k > 1:
            val = val + self.zmr[k - 2].astype(F32)
        self.zms[k - 1] = val.astype(BF16)
        self.copy("m%d" % k, k, self.zms.at[k - 1], self.zmr.at[k - 1], self.here.at(dz=-way))
        if k <= 3:
            if k > 1:
                self.copies["p%d" % (k - 1)].wait_recv()
            val = self.local((z + way * (4 - k) + NZ) % NZ)
            if k > 1:
                val = val + self.zpr[k - 2].astype(F32)
            self.zps[k - 1] = val.astype(BF16)
            self.copy("p%d" % k, 4 + k, self.zps.at[k - 1], self.zpr.at[k - 1], self.here.at(dz=way))

    def ycopy(self):
        d = (self.target - self.here.y + NY) % NY
        slot = (d - 1 + NY) % NY
        return d, remote(
            self.ysend, self.yrecv.at[slot], self.ssem.at[8], self.ysem.at[slot],
            ((self.target * NZ + self.here.z) * 2 + self.here.c, self.here.x),
        )

    def last(self):
        self.copies["m4"].wait_recv()
        self.copies["p3"].wait_recv()
        val = self.local(self.here.z) + self.zmr[3].astype(F32) + self.zpr[2].astype(F32)
        d, made = self.ycopy()

        @pl.when(d == 0)
        def _():
            self.keep[...] = val

        @pl.when(d != 0)
        def _():
            self.ysend[...] = val.astype(BF16)
            made.start()

    def finish(self):
        for made in self.copies.values():
            made.wait_send()
        d, made = self.ycopy()

        @pl.when(d != 0)
        def _():
            made.wait_send()


def kernel(scale, factor, q_hbm, k_hbm, v_hbm, og_hbm, w_hbm, dq_hbm, dk_hbm, dv_hbm, dw_hbm,
           q, k, v, w, og, probs, opart, o, dacc, do, dkacc, dvacc, dq_ref, dk_ref, dv_ref, dw_ref,
           lsem, osem, xssem, xrsem, *rest):
    here = Place()
    rows = q.shape[0]
    half = rows // 2
    heads = q.shape[1] // HD
    scan_k = Scan(here, rest[0:12], True)
    scan_b = Scan(here, rest[12:24], False)
    red_refs = rest[24:]
    upper = here.z >= NZ // 2
    side = jnp.where(upper, 1, -1)
    targets = [here.x, (here.x + side + NX) % NX, (here.x - side + NX) % NX, (here.x + 2) % NX]
    units = [Reduce(here, u, targets[u], red_refs) for u in range(4)]

    loads = [pltpu.make_async_copy(src, dst, lsem.at[n]) for n, (src, dst) in enumerate(
        [(k_hbm, k), (v_hbm, v), (q_hbm, q)]
        + [(og_hbm.at[:, pl.ds(i * half * 2, half * 2)], og.at[0, i]) for i in range(2)]
        + [(w_hbm, w)])]
    for made in loads:
        made.start()

    barrier = pltpu.get_barrier_semaphore()
    peers = [here.at(flip=True), here.at(dx=1), here.at(dx=-1), here.at(dz=1), here.at(dz=-1),
             here.at(dy=1), here.at(dy=2), here.at(dy=3)]
    for peer in peers:
        pl.semaphore_signal(barrier, inc=1, device_id=peer, device_id_type=MESH)
    pl.semaphore_wait(barrier, len(peers))

    cols = [pl.ds(i * half * 2, half * 2) for i in range(2)]
    right, left = here.at(dx=1), here.at(dx=-1)

    def xcopy(n, src, dst, device):
        return remote(src, dst, xssem.at[n], xrsem.at[n], device)

    x0 = xcopy(0, og_hbm.at[:, cols[0]], og.at[1, 0], right)
    x1 = xcopy(1, og_hbm.at[:, cols[1]], og.at[2, 1], left)
    x2 = xcopy(2, og_hbm.at[:, cols[0]], og.at[2, 0], left)
    x3 = xcopy(3, og_hbm.at[:, cols[1]], og.at[1, 1], right)
    x4 = xcopy(4, og.at[1, 0], og.at[3, 0], right)
    x5 = xcopy(5, og.at[2, 1], og.at[3, 1], left)
    for made in (x0, x1, x2, x3):
        made.start()

    def hc(h):
        return slice(h * HD, (h + 1) * HD)

    def blk(i):
        return slice(i * half, (i + 1) * half)

    def masked(s, i):
        t = lax.broadcasted_iota(jnp.int32, s.shape, 0) + i * half
        u = lax.broadcasted_iota(jnp.int32, s.shape, 1)
        return jnp.where(u <= t, s * scale, 0.0).astype(BF16)

    def p_head(h):
        for i in range(2):
            n = (i + 1) * half
            p = masked(dotg(q[blk(i), hc(h)], k[0:n, hc(h)], 1, 1), i)
            probs[h, blk(i), 0:n] = p
            opart[blk(i), hc(h)] = jnp.dot(p, v[0:n, hc(h)], preferred_element_type=F32)

    def g_head(h):
        g0 = masked(dotg(do[blk(0), hc(h)], v[0:half, hc(h)], 1, 1), 0)
        g1 = masked(dotg(do[blk(1), hc(h)], v[:, hc(h)], 1, 1), 1)
        prior = scan_k.out[h]
        a = jnp.dot(g0, k[0:half, hc(h)], preferred_element_type=F32)
        dq_ref[blk(0), hc(h)] = (a + dotg(do[blk(0), hc(h)], prior, 1, 1)).astype(BF16)
        a = jnp.dot(g1, k[:, hc(h)], preferred_element_type=F32)
        dq_ref[blk(1), hc(h)] = (a + dotg(do[blk(1), hc(h)], prior, 1, 1)).astype(BF16)
        dkacc[blk(0), hc(h)] = dotg(g0, q[blk(0), hc(h)], 0, 0) + dotg(g1[:, 0:half], q[blk(1), hc(h)], 0, 0)
        dkacc[blk(1), hc(h)] = dotg(g1[:, half:], q[blk(1), hc(h)], 0, 0)
        dvacc[blk(0), hc(h)] = dotg(probs[h, :, 0:half], do[:, hc(h)], 0, 0)
        dvacc[blk(1), hc(h)] = dotg(probs[h, blk(1), half:], do[blk(1), hc(h)], 0, 0)

    def wrow(shift, i):
        return ((here.x + shift + NX) % NX) * 2 + i

    chunks = [((0, 0, 0), (0, 1, 0)), ((1, 0, -1), (2, 1, 1)), ((2, 0, 1), (1, 1, -1)), ((3, 0, 2), (3, 1, 2))]

    def do_unit(u):
        for i in range(2):
            acc = None if u == 0 else dacc[blk(i), :]
            for slot, part, shift in chunks[u]:
                a = jnp.dot(og[slot, part, blk(i), :], w[wrow(shift, part)], preferred_element_type=F32)
                acc = a if acc is None else acc + a
            if u == 3:
                do[blk(i), :] = acc.astype(BF16)
            else:
                dacc[blk(i), :] = acc

    def product(u):
        for slot, part, _ in chunks[u]:
            for i in range(2):
                a = dotg(og[slot, part, :, blk(i)], o[...], 0, 0)
                units[u].prod[pl.ds(part * 4 + i * 2, 2)] = a.reshape(2, 2, 64, rows).astype(BF16)
            units[u].core_start(part)

    def store(n, src, dst):
        made = pltpu.make_async_copy(src, dst, osem.at[n])
        made.start()
        return made

    for made in loads[:2]:
        made.wait()
    for h in range(heads):
        scan_k.term[h] = scale * dotg(k[:, hc(h)], v[:, hc(h)], 0, 0)
    scan_k.p1_start(0)
    scan_k.p1_start(1)
    loads[2].wait()
    scan_k.z_step(1)
    p_head(0)
    scan_k.z_step(2)
    p_head(1)
    scan_k.z_step(3)
    p_head(2)
    scan_k.z_step(4)
    p_head(3)
    scan_k.y_start(0)
    scan_k.y_start(1)
    for made in loads[3:]:
        made.wait()
    do_unit(0)
    scan_k.f_start(0)
    scan_k.f_start(1)
    x0.wait_recv()
    x4.start()
    x1.wait_recv()
    x5.start()
    scan_k.f_wait()
    for h in range(heads):
        a = jnp.dot(q[:, hc(h)], scan_k.out[h], preferred_element_type=F32)
        o[:, hc(h)] = (opart[:, hc(h)] + a).astype(BF16)
    product(0)
    product(1)
    units[0].step(1)
    do_unit(1)
    units[1].step(1)
    x2.wait_recv()
    x3.wait_recv()
    product(2)
    units[0].step(2)
    units[1].step(2)
    do_unit(2)
    units[2].step(1)
    units[0].step(3)
    units[1].step(3)
    units[2].step(2)
    x4.wait_recv()
    x5.wait_recv()
    do_unit(3)
    for h in range(heads):
        scan_b.term[h] = scale * dotg(q[:, hc(h)], do[:, hc(h)], 0, 0)
    scan_b.p1_start(0)
    scan_b.p1_start(1)
    units[0].step(4)
    units[1].step(4)
    scan_b.z_step(1)
    product(3)
    units[2].step(3)
    scan_b.z_step(2)
    g_head(0)
    units[3].step(1)
    units[0].last()
    units[1].last()
    scan_b.z_step(3)
    units[2].step(4)
    g_head(1)
    units[3].step(2)
    scan_b.z_step(4)
    g_head(2)
    units[3].step(3)
    scan_b.y_start(0)
    scan_b.y_start(1)
    g_head(3)
    stores = [store(0, dq_ref, dq_hbm)]
    units[2].last()
    units[3].step(4)
    scan_b.f_start(0)
    scan_b.f_start(1)
    units[3].last()
    scan_b.f_wait()
    for h in range(heads):
        later = scan_b.out[h]
        dk_ref[:, hc(h)] = (dkacc[:, hc(h)] + dotg(v[:, hc(h)], later, 1, 1)).astype(BF16)
        a = jnp.dot(k[:, hc(h)], later, preferred_element_type=F32)
        dv_ref[:, hc(h)] = (dvacc[:, hc(h)] + a).astype(BF16)
        if h % 2 == 1:
            pair = pl.ds((h - 1) * HD, 2 * HD)
            stores.append(store(1 + h // 2 * 3, dk_ref.at[:, pair], dk_hbm.at[:, pair]))
            stores.append(store(2 + h // 2 * 3, dv_ref.at[:, pair], dv_hbm.at[:, pair]))
    total = units[0].keep[...]
    for d in range(NY - 1):
        remote(units[0].ysend, units[0].yrecv.at[d], units[0].ssem.at[8], units[0].ysem.at[d], here.at(dy=1)).wait_recv()
        total = total + units[0].yrecv[d].astype(F32)
    dw_ref[...] = total * factor
    stores.append(store(3, dw_ref, dw_hbm))
    for made in (x0, x1, x2, x3, x4, x5):
        made.wait_send()
    scan_k.finish()
    scan_b.finish()
    for unit in units:
        unit.finish()
    for made in stores:
        made.wait()


def settle(*refs):
    n = (len(refs) - 1) // 3
    ins, outs, held, sem = refs[:n], refs[n:2 * n], refs[2 * n:3 * n], refs[3 * n]
    first = [pltpu.make_async_copy(ins[i], held[i], sem.at[0, i]) for i in range(n)]
    second = [pltpu.make_async_copy(held[i], outs[i], sem.at[1, i]) for i in range(n)]
    for made in first:
        made.start()
    for a, b in zip(first, second):
        a.wait()
        b.start()
    for made in second:
        made.wait()


def per_device(queries, keys, values, out_grad, out_weight):
    rows, width = queries.shape
    feat = out_grad.shape[1]
    total = lax.axis_size("seq") * rows
    scale = 1.0 / math.sqrt(HD * total)
    factor = 1.0 / math.sqrt(total)
    heads = width // HD
    part = feat // 2
    blocks = out_weight.shape[0] // part
    out_rows = out_weight.shape[0] // lax.axis_size("seq")
    sem = pltpu.SemaphoreType.DMA
    n = heads // 2

    def scan(dtype):
        return [
            pltpu.VMEM((heads, HD, HD), F32), pltpu.VMEM((n, HD, HD), F32), pltpu.VMEM((n, HD, HD), dtype),
            pltpu.VMEM((n, 4, HD, HD), dtype), pltpu.VMEM((n, 3, HD, HD), dtype), pltpu.VMEM((n, HD, HD), dtype),
            pltpu.VMEM((n, 3, HD, HD), dtype), pltpu.VMEM((n, HD, HD), BF16), pltpu.VMEM((heads, HD, HD), BF16),
            pltpu.VMEM((n, HD, HD), F32), sem((n, 12)), sem((n, 12)),
        ]

    reduce = [
        pltpu.VMEM((4, NZ, 2, out_rows, width), BF16), pltpu.VMEM((4, NZ, out_rows, width), BF16),
        pltpu.VMEM((4, 4, out_rows, width), BF16), pltpu.VMEM((4, 4, out_rows, width), BF16),
        pltpu.VMEM((4, 3, out_rows, width), BF16), pltpu.VMEM((4, 3, out_rows, width), BF16),
        pltpu.VMEM((4, out_rows, width), BF16), pltpu.VMEM((3, out_rows, width), BF16),
        pltpu.VMEM((out_rows, width), F32), sem((4, 10)), sem((4, 10)), sem((3,)),
    ]
    hbm = pl.BlockSpec(memory_space=pl.ANY)
    grad = jax.ShapeDtypeStruct((rows, width), BF16)
    outs = (grad, grad, grad, jax.ShapeDtypeStruct((out_rows, width), F32))
    held = [pltpu.VMEM(a.shape, a.dtype) for a in outs]
    results = pl.pallas_call(
        functools.partial(kernel, scale, factor),
        out_shape=outs,
        in_specs=[hbm] * 5,
        out_specs=[hbm] * 4,
        scratch_shapes=[
            pltpu.VMEM((rows, width), BF16), pltpu.VMEM((rows, width), BF16), pltpu.VMEM((rows, width), BF16),
            pltpu.VMEM((blocks, part, width), BF16), pltpu.VMEM((4, 2, rows, part), BF16),
            pltpu.VMEM((heads, rows, rows), BF16), pltpu.VMEM((rows, width), F32), pltpu.VMEM((rows, width), BF16),
            pltpu.VMEM((rows, width), F32), pltpu.VMEM((rows, width), BF16),
            pltpu.VMEM((rows, width), F32), pltpu.VMEM((rows, width), F32),
        ] + held + [sem((6,)), sem((6,)), sem((6,)), sem((6,))] + scan(BF16) + scan(BF16) + reduce,
        compiler_params=pltpu.CompilerParams(
            collective_id=0, has_side_effects=True, vmem_limit_bytes=60 * 1024 * 1024
        ),
        name="attention_backward",
    )(queries, keys, values, out_grad, out_weight.reshape(blocks, part, width))
    return pl.pallas_call(
        settle,
        out_shape=outs,
        in_specs=[hbm] * 4,
        out_specs=[hbm] * 4,
        scratch_shapes=held + [sem((2, 4))],
        name="settle",
    )(*results)


def solution(mesh):
    return jax.shard_map(
        per_device,
        mesh=mesh,
        in_specs=(P("seq", "head"), P("seq", "head"), P("seq", "head"), P("seq", "head"), P(None, "head")),
        out_specs=(P("seq", "head"), P("seq", "head"), P("seq", "head"), P("seq", "head")),
        check_vma=False,
    )
```
